32 devices in a mesh: seq: 4 (over z), ctx: 8 (over y, x, core).
Axes of the slice: x: 2, y: 2, z: 4, core: 2. Of those that a mesh axis runs over, the one named last changes fastest.
Arguments:
- tokens: bfloat16 [4, 1024, 1600], P('seq', 'ctx'), may hold values from -10 to 10, as said below
- cotangent: bfloat16 [4, 1024, 1600], P('seq', 'ctx'), may hold values from -6 to 6
- segments: int32 [4, 1024], P('seq'), may hold values from 0 to 3, never falling along the last dimension, each value on 1 to 512 neighbouring positions
- block_order: int32 [16], replicated, may hold values from 0 to 15, each once
- w_attn: bfloat16 [1600, 4800], P('seq', 'ctx'), may hold values from -0.15625 to 0.15625
- w_proj: bfloat16 [1600, 1600], P('seq', 'ctx'), may hold values from -1.25 to 1.25
- w_fc: bfloat16 [1600, 6400], P('seq', 'ctx'), may hold values from -0.15625 to 0.15625
- w_fc2: bfloat16 [6400, 1600], P('seq', 'ctx'), may hold values from -0.078125 to 0.078125
- attn_vectors: bfloat16 [6400], P(('seq', 'ctx')), may hold values from -2 to 2, as said below
- other_vectors: bfloat16 [12800], P(('seq', 'ctx')), may hold values from -2 to 2, as said below
Outputs:
- output: bfloat16 [4, 1024, 1600], P('seq', 'ctx')
- tokens_grad: bfloat16 [4, 1024, 1600], P('seq', 'ctx')
- w_attn_grad: float32 [1600, 4800], P('seq', 'ctx')
- w_proj_grad: float32 [1600, 1600], P('seq', 'ctx')
- w_fc_grad: float32 [1600, 6400], P('seq', 'ctx')
- w_fc2_grad: float32 [6400, 1600], P('seq', 'ctx')
- attn_vectors_grad: float32 [6400], P(('seq', 'ctx'))
- other_vectors_grad: float32 [12800], P(('seq', 'ctx'))
The draws below stay inside these ranges and needn't reach their ends.
Inputs may be any that keep to these rules, and one draw needn't show every extreme that they name: `tokens`: activations of order one whose rows and columns have different scales. `attn_vectors`: gains near one and biases of order one or smaller. `other_vectors`: gains near one and biases of order one or smaller.
All inputs are finite; a program needn't handle non-finite values.
Results may differ from the reference program's by a relative error of at most 0.015.
Values may be sent and summed in bfloat16 or wider, within the bound.
No kernel may reach another device: no remote copies, remote signals or barrier semaphores. Data moves between devices by JAX's collectives and lax.ppermute only.
A program may use at most 320 MiB of HBM per device.

```python
import math
import jax
import jax.numpy as jnp
import numpy as np
from jax import lax

D = 1600
FF = 6400
H = 25
HD = 64
SEQUENCES = 4
LENGTH = 1024
SEG_MOST = 512
SEGS = 4
VEC_ATTN = 6400
VEC_REST = 12800
N_CTX = 8


def draw_tokens(key, part):
    subkeys = jax.random.split(key, 3)
    shape_all = (SEQUENCES, LENGTH, D)
    row_scale = jnp.exp(jax.random.uniform(subkeys[1], (SEQUENCES, LENGTH, 1), jnp.float32, math.log(0.5), math.log(2.0)))
    column_scale = jnp.exp(jax.random.uniform(subkeys[2], (1, 1, D), jnp.float32, math.log(0.7), math.log(1.4)))
    normal_part = jax.random.truncated_normal(subkeys[0], -3.0, 3.0, shape_all, jnp.float32)
    return (normal_part * row_scale * column_scale).astype(jnp.bfloat16)


def gains_and_biases(key, count, gain_start):
    subkeys = jax.random.split(key, 2)
    position = jnp.arange(count)
    is_gain = (position >= gain_start) & (position < gain_start + D)
    gain_values = 1.0 + 0.15 * jax.random.truncated_normal(subkeys[0], -3.0, 3.0, (count,), jnp.float32)
    biases = 0.3 * jax.random.truncated_normal(subkeys[1], -3.0, 3.0, (count,), jnp.float32)
    return jnp.where(is_gain, gain_values, biases)


def draw_attn_vectors(key, part):
    return gains_and_biases(jax.random.fold_in(key, 11), VEC_ATTN, 0).astype(jnp.bfloat16)


def draw_other_vectors(key, part):
    return gains_and_biases(jax.random.fold_in(key, 23), VEC_REST, D).astype(jnp.bfloat16)


def block_scale(rng, dims, cuts, low, high):
    loudness, own = 1.0, jax.random.fold_in(rng, 6)
    for axis_at, parts in cuts:
        draws = jnp.exp(jax.random.uniform(jax.random.fold_in(own, axis_at), (parts,), jnp.float32, low / len(cuts), high / len(cuts)))
        loudness = loudness * jnp.repeat(draws, dims[axis_at] // parts).reshape([-1 if axis == axis_at else 1 for axis in range(len(dims))])
    return loudness


def profile(amount, total, reach, slope):
    portions = [(1 << 20) // math.isqrt(grade ** slope) + 1 for grade in range(2, amount + 1)]
    surplus, given = total - reach - (amount - 1), [1] * (amount - 1)
    while surplus > 0:
        free = [i for i in range(amount - 1) if given[i] < reach]
        whole, remaining = sum([portions[i] for i in free]), surplus
        for i in free:
            more = min(reach - given[i], max(1, remaining * portions[i] // whole), surplus)
            given[i] = given[i] + more
            surplus = surplus - more
    return np.array([reach] + given)


def uneven_parts(stream_key, count, total, bound, slope):
    if count == 2:
        one = jax.random.randint(stream_key, (), max(1, total - bound), min(bound, total - 1) + 1)
        return jnp.stack([one, total - one])
    sizes = jnp.asarray(profile(count, total, bound, slope), jnp.int32)
    pairs = (count - 1) // 2
    source_of, taker = sizes[1:1 + 2 * pairs:2], sizes[2:2 + 2 * pairs:2]
    slack = jnp.minimum(source_of - 1, bound - taker)
    moved = jax.random.randint(jax.random.fold_in(stream_key, 1), (pairs,), 0, 1 << 20) % (slack + 1)
    sizes = sizes.at[1:1 + 2 * pairs:2].set(source_of - moved).at[2:2 + 2 * pairs:2].set(taker + moved)
    return sizes[jax.random.permutation(jax.random.fold_in(stream_key, 2), count)]


def normal_values(stream_key, extent, width, most, shards=(), kind=jnp.bfloat16):
    array = width * jax.random.normal(stream_key, extent, jnp.float32)
    if shards:
        array = array * block_scale(stream_key, extent, shards, -0.22, 0.18)
    return jnp.clip(array, -most, most).astype(kind)


def setup_inputs(seed: int = 0) -> dict:
    key_list = jax.random.split(jax.random.key(seed), 11)
    return {
        "tokens": draw_tokens(jax.random.fold_in(key_list[10], 71), 0),
        "cotangent": normal_values(key_list[1], (SEQUENCES, LENGTH, D), 1.0, 6.0, ((0, 4), (1, 8))),
        "segments": jax.vmap(lambda own: jnp.searchsorted(jnp.cumsum(uneven_parts(own, SEGS, LENGTH, SEG_MOST, 2)), jnp.arange(LENGTH), side="right"))(jax.random.split(key_list[2], SEQUENCES)).reshape((SEQUENCES, LENGTH)).astype(jnp.int32),
        "block_order": jax.random.permutation(key_list[3], 2 * N_CTX).astype(jnp.int32),
        "w_attn": normal_values(key_list[4], (D, 3 * D), D ** -0.5, 0.15625, ((0, 4), (1, 8))),
        "w_proj": normal_values(key_list[5], (D, D), (D // 64) ** -0.5, 1.25, ((0, 4), (1, 8))),
        "w_fc": normal_values(key_list[6], (D, FF), D ** -0.5, 0.15625, ((0, 4), (1, 8))),
        "w_fc2": normal_values(key_list[7], (FF, D), FF ** -0.5, 0.078125, ((0, 4), (1, 8))),
        "attn_vectors": draw_attn_vectors(jax.random.fold_in(key_list[10], 71), 0),
        "other_vectors": draw_other_vectors(jax.random.fold_in(key_list[10], 71), 0),
    }


@jax.custom_vjp
def low(v):
    return lax.optimization_barrier(v.astype(jnp.bfloat16)).astype(jnp.float32)

@jax.custom_vjp
def low_back(v):
    return v

def low_keep(v):
    return (low(v), None)

def low_pass(kept, grad):
    return (grad,)

def back_keep(v):
    return (v, None)

def back_low(kept, grad):
    return (low(grad),)
low.defvjp(low_keep, low_pass)
low_back.defvjp(back_keep, back_low)

def layer_norm(values, norm_gain, norm_shift):
    average = lax.optimization_barrier(jnp.mean(values, axis=-1, keepdims=True))
    centred = values - average
    spread = lax.optimization_barrier(jnp.mean(centred * centred, axis=-1, keepdims=True))
    return centred * lax.rsqrt(spread + 1e-05) * norm_gain + norm_shift

def gelu_tanh(inner_sum):
    return 0.5 * inner_sum * (1.0 + jnp.tanh(0.7978845608028654 * (inner_sum + 0.044715 * inner_sum * inner_sum * inner_sum)))

def attention(queries, keys_all, values_all, places, labels):
    length = queries.shape[0]
    block_rows = min(512, length)
    blocks = length // block_rows
    key_heads = keys_all.reshape(length, H, HD)
    value_heads = values_all.reshape(length, H, HD)
    query_blocks = queries.reshape(blocks, block_rows, H, HD)
    place_blocks = places.reshape(blocks, block_rows)
    label_blocks = labels.reshape(blocks, block_rows)

    def single(packed):
        query_part, place_part, label_part = packed
        scores = jnp.einsum('qhd,khd->hqk', query_part, key_heads, precision=lax.Precision.HIGHEST) * 0.125
        allowed = (places[None, :] <= place_part[:, None]) & (labels[None, :] == label_part[:, None])
        scores = low_back(jnp.where(allowed[None], scores, -1e+30))
        highest = lax.optimization_barrier(jnp.max(scores, axis=-1, keepdims=True))
        log_total = highest + jnp.log(lax.optimization_barrier(jnp.sum(jnp.exp(scores - highest), axis=-1, keepdims=True)))
        probabilities = low(jnp.exp(scores - log_total))
        mixture = jnp.einsum('hqk,khd->qhd', probabilities, value_heads, precision=lax.Precision.HIGHEST)
        return mixture.reshape(block_rows, H * HD)
    mixed_all = lax.map(jax.checkpoint(single), (query_blocks, place_blocks, label_blocks))
    return mixed_all.reshape(length, H * HD)

def block_layer(stream, w_attn, w_proj, w_fc, w_fc2, attn_vectors, other_vectors, places, labels):
    pieces = [attn_vectors[number * D:(number + 1) * D] for number in range(4)]
    pieces = pieces + [other_vectors[number * D:(number + 1) * D] for number in range(4)]
    bias_fc = other_vectors[4 * D:]
    normed_one = low(layer_norm(stream, pieces[0], pieces[1]))
    bias_joined = jnp.concatenate([pieces[2], jnp.zeros_like(pieces[2]), pieces[3]])
    joined_qkv = low(low_back(jnp.dot(normed_one, w_attn, precision=lax.Precision.HIGHEST) + bias_joined))
    attended = attention(joined_qkv[:, :D], joined_qkv[:, D:2 * D], joined_qkv[:, 2 * D:], places, labels)
    attended = low(low_back(attended))
    middle = stream + low_back(jnp.dot(attended, w_proj, precision=lax.Precision.HIGHEST)) + pieces[4]
    normed_two = low(layer_norm(middle, pieces[5], pieces[6]))
    inner_sum = low_back(jnp.dot(normed_two, w_fc, precision=lax.Precision.HIGHEST) + bias_fc)
    active = low(gelu_tanh(inner_sum))
    return middle + jnp.dot(active, w_fc2, precision=lax.Precision.HIGHEST) + pieces[7]

def reference(tokens, cotangent, segments, block_order, w_attn, w_proj, w_fc, w_fc2, attn_vectors, other_vectors):
    length = tokens.shape[1]
    half_block = length // (2 * N_CTX)
    stored = jnp.arange(length, dtype=jnp.int32)
    places = (jnp.take(block_order, stored // half_block).astype(jnp.int32) * half_block + stored % half_block).astype(jnp.int32)
    labels = jnp.take(segments, places, axis=1).astype(jnp.int32)

    def forward(stream, attn_weight, proj_weight, fc_weight, out_weight, first_vector, second_vector):

        def per_row(packed):
            return block_layer(packed[0], attn_weight, proj_weight, fc_weight, out_weight, first_vector, second_vector, places, packed[1])
        return lax.map(per_row, (stream, labels))
    result, pullback = jax.vjp(forward, tokens.astype(jnp.float32), w_attn.astype(jnp.float32), w_proj.astype(jnp.float32), w_fc.astype(jnp.float32), w_fc2.astype(jnp.float32), attn_vectors.astype(jnp.float32), other_vectors.astype(jnp.float32))
    gradients = pullback(cotangent.astype(jnp.float32))
    return (result.astype(jnp.bfloat16), gradients[0].astype(jnp.bfloat16), gradients[1], gradients[2], gradients[3], gradients[4], gradients[5], gradients[6])
```

```python
import jax
import jax.numpy as jnp
from jax import lax
from jax.sharding import PartitionSpec as P

D = 1600
FF = 6400
H = 25
HD = 64
BF = jnp.bfloat16
F32 = jnp.float32


def mm(a, b):
    return jnp.dot(a, b, preferred_element_type=F32)


def mm_nt(a, b):
    return lax.dot_general(a, b, (((1,), (1,)), ((), ())), preferred_element_type=F32)


def mm_tn(a, b):
    return lax.dot_general(a, b, (((0,), (0,)), ((), ())), preferred_element_type=F32)


def swap(value, step):
    count = lax.axis_size("ctx")
    return lax.ppermute(value, "ctx", [(i, i ^ step) for i in range(count)])


def local_order(count):
    return list(range(0, count, 2)) + list(range(1, count, 2))


def gather_blocks(own):
    count = lax.axis_size("ctx")
    even = [own] + [swap(own, step) for step in range(2, count, 2)]
    odd = [swap(block, 1) for block in even]
    return even + odd


def gather_rows(own):
    return jnp.concatenate(gather_blocks(own), axis=0)


def scatter_sum(left, right_weight, product):
    count = lax.axis_size("ctx")
    half = left.shape[0] // 2
    rows = left.shape[0] // count
    other = product(left[half:], right_weight).astype(BF)
    mine = product(left[:half], right_weight)
    mine = mine + swap(other, 1).astype(F32)
    total = mine[:rows]
    for number in range(1, count // 2):
        block = mine[number * rows : (number + 1) * rows].astype(BF)
        total = total + swap(block, 2 * number).astype(F32)
    return total


def pick(stack, number):
    return lax.dynamic_index_in_dim(stack, number, 0, keepdims=False)


def exchange(blocks_by_owner):
    count = lax.axis_size("ctx")
    me = lax.axis_index("ctx")
    got = jnp.stack([swap(pick(blocks_by_owner, me ^ step), step) if step else pick(blocks_by_owner, me) for step in range(count)])
    return [pick(got, me ^ sender) for sender in range(count)]


def hidden_forward(w_fc, unit):
    seqs, count = lax.axis_size("seq"), lax.axis_size("ctx")
    assert count == 2 * seqs
    me = lax.axis_index("ctx")
    stack = jnp.stack([w_fc[:, k * unit : (k + 1) * unit] for k in range(seqs)])
    got = []
    for step in range(seqs):
        pairs = [(2 * (v ^ step) + u, seqs * u + v) for u in range(2) for v in range(seqs)]
        got.append(lax.ppermute(pick(stack, (me // 2) ^ step), "ctx", pairs))
    got = jnp.stack(got)
    return jnp.concatenate([pick(got, (me % seqs) ^ k) for k in range(seqs)], axis=1)


def hidden_backward(grad, unit):
    seqs = lax.axis_size("seq")
    me = lax.axis_index("ctx")
    stack = jnp.stack([grad[:, k * unit : (k + 1) * unit] for k in range(seqs)])
    got = []
    for step in range(seqs):
        pairs = [(seqs * u + v, 2 * (v ^ step) + u) for u in range(2) for v in range(seqs)]
        got.append(lax.ppermute(pick(stack, (me % seqs) ^ step), "ctx", pairs))
    got = jnp.stack(got)
    return jnp.concatenate([pick(got, (me // 2) ^ k) for k in range(seqs)], axis=1)


def gelu_and_grad(a):
    inner = 0.7978845608028654 * (a + 0.044715 * a * a * a)
    t = jnp.tanh(inner)
    value = 0.5 * a * (1.0 + t)
    slope = 0.5 * (1.0 + t) + 0.5 * a * (1.0 - t * t) * 0.7978845608028654 * (1.0 + 3 * 0.044715 * a * a)
    return value, slope


def normalize(values):
    average = jnp.mean(values, axis=-1, keepdims=True)
    centred = values - average
    scale = lax.rsqrt(jnp.mean(centred * centred, axis=-1, keepdims=True) + 1e-05)
    return centred * scale, scale


def norm_back(grad, gain, normed, scale):
    e = grad * gain
    return scale * (
        e - jnp.mean(e, axis=-1, keepdims=True) - normed * jnp.mean(e * normed, axis=-1, keepdims=True)
    )


def body(tokens, cotangent, segments, block_order, w_attn, w_proj, w_fc, w_fc2, attn_vectors, other_vectors):
    seqs, count = lax.axis_size("seq"), lax.axis_size("ctx")
    me = lax.axis_index("ctx")
    rows = tokens.shape[1]
    length = rows * count
    half_block = rows // 2
    heads = -(-H // count)
    width = heads * HD
    unit = FF // (seqs * count)
    order = local_order(count)

    attn_cols = w_attn.shape[1]
    attn_blocks = gather_blocks(w_attn)
    wanted = jnp.arange(width, dtype=jnp.int32) + me * width
    wanted = jnp.concatenate([jnp.where(wanted < D, wanted + part * D, -1) for part in range(3)])

    def chosen(owner):
        return (jnp.arange(attn_cols, dtype=jnp.int32)[:, None] + owner * attn_cols) == wanted[None, :]

    attn_part = sum(mm(block, chosen(me ^ b).astype(BF)) for b, block in zip(order, attn_blocks)).astype(BF)
    proj_cols = w_proj.shape[1]
    proj_all = lax.all_gather(w_proj, "seq", axis=0, tiled=True)
    attn_mine = lax.all_gather(attn_part, "seq", axis=0, tiled=True)
    fc_mine = lax.all_gather(hidden_forward(w_fc, unit), "seq", axis=0, tiled=True)
    out_blocks = exchange(w_fc2.reshape(count, unit, w_fc2.shape[1]))
    out_mine = lax.all_gather(jnp.concatenate(out_blocks, axis=1), "seq", axis=0, tiled=True)
    proj_pad = jnp.pad(proj_all, ((0, count * width - D), (0, 0))).reshape(count, width, proj_cols)
    proj_mine = jnp.concatenate(exchange(proj_pad), axis=1)

    vectors = lax.all_gather(jnp.concatenate([attn_vectors, other_vectors]), ("seq", "ctx"), axis=0, tiled=False)
    first_all = vectors[:, : attn_vectors.shape[0]].reshape(-1).astype(F32)
    second_all = vectors[:, attn_vectors.shape[0] :].reshape(-1).astype(F32)
    gain_one, shift_one, bias_query, bias_value = [first_all[n * D : (n + 1) * D] for n in range(4)]
    bias_proj, gain_two, shift_two, bias_out = [second_all[n * D : (n + 1) * D] for n in range(4)]
    bias_fc = pick(second_all[4 * D :].reshape(seqs, count, unit).transpose(1, 0, 2), me).reshape(-1)

    def my_heads(vector):
        return lax.dynamic_slice_in_dim(jnp.pad(vector, (0, count * width - D)), me * width, width)

    x_own = tokens[0].astype(F32)
    x_all = gather_rows(tokens[0]).astype(F32)
    normed_one, _ = normalize(x_all)
    h1 = (normed_one * gain_one + shift_one).astype(BF)
    bias_joined = jnp.concatenate([my_heads(bias_query), jnp.zeros((width,), F32), my_heads(bias_value)])
    qkv = (mm(h1, attn_mine) + bias_joined).astype(BF)

    owners = jnp.stack([me ^ b for b in order])
    stored = (owners[:, None] * 2 + jnp.arange(2, dtype=jnp.int32)[None, :]).reshape(-1)
    blocks = jnp.take(block_order, stored)
    places = (blocks[:, None] * half_block + jnp.arange(half_block, dtype=jnp.int32)[None, :]).reshape(-1)
    labels = jnp.take(segments[0].reshape(-1, half_block), blocks, axis=0).reshape(-1)
    allowed = (places[None, :] <= places[:, None]) & (labels[None, :] == labels[:, None])

    def split(value):
        return value.reshape(length, heads, HD).transpose(1, 0, 2)

    q = split(qkv[:, :width]) * BF(0.125)
    k = split(qkv[:, width : 2 * width])
    v = split(qkv[:, 2 * width :])
    scores = jnp.einsum("hqd,hkd->hqk", q, k, preferred_element_type=F32)
    scores = jnp.where(allowed[None], scores, -1e30)
    highest = jnp.max(scores, axis=-1, keepdims=True)
    weights = jnp.exp(scores - highest)
    total = jnp.sum(weights, axis=-1, keepdims=True)
    lse = highest + jnp.log(total)
    mixed = jnp.einsum("hqk,hkd->hqd", weights.astype(BF), v, preferred_element_type=F32) / total
    attended = mixed.transpose(1, 0, 2).reshape(length, width).astype(BF)
    middle = x_own + scatter_sum(attended, proj_mine, mm) + bias_proj
    normed_two, scale_two = normalize(middle)
    h2 = gather_rows((normed_two * gain_two + shift_two).astype(BF))
    inner = mm(h2, fc_mine) + bias_fc
    active, slope = gelu_and_grad(inner)
    active = active.astype(BF)
    output = (middle + scatter_sum(active, out_mine, mm) + bias_out).astype(BF)

    dy_own = cotangent[0].astype(F32)
    dy = gather_rows(cotangent[0])
    grad_inner = (mm_nt(dy, out_mine) * slope).astype(BF)
    grad_out_w = mm_tn(active, dy).astype(BF)
    grad_fc_w = mm_tn(h2, grad_inner).astype(BF)
    out_sum = lax.psum_scatter(grad_out_w, "seq", scatter_dimension=0, tiled=True)
    fc_sum = lax.psum_scatter(grad_fc_w, "seq", scatter_dimension=0, tiled=True)
    grad_h2 = scatter_sum(grad_inner, fc_mine, mm_nt)
    grad_middle = dy_own + norm_back(grad_h2, gain_two, normed_two, scale_two)
    r_all = gather_rows(grad_middle.astype(BF))
    grad_proj_w = mm_tn(attended, r_all).astype(BF)
    proj_sent = jnp.stack([grad_proj_w[:, c * proj_cols : (c + 1) * proj_cols] for c in range(count)])
    proj_part = jnp.concatenate(exchange(proj_sent), axis=0)[:D]
    proj_own = lax.psum_scatter(proj_part, "seq", scatter_dimension=0, tiled=True).astype(F32)

    grad_heads = split(mm_nt(r_all, proj_mine).astype(BF))
    prob = jnp.exp(scores - lse)
    grad_v = jnp.einsum("hqk,hqd->hkd", prob.astype(BF), grad_heads, preferred_element_type=F32)
    grad_prob = jnp.einsum("hqd,hkd->hqk", grad_heads, v, preferred_element_type=F32)
    delta = jnp.sum(grad_heads.astype(F32) * mixed, axis=-1, keepdims=True)
    grad_scores = (prob * (grad_prob - delta)).astype(BF)
    grad_q = jnp.einsum("hqk,hkd->hqd", grad_scores, k, preferred_element_type=F32) * 0.125
    grad_k = jnp.einsum("hqk,hqd->hkd", grad_scores, q, preferred_element_type=F32)

    def join(value):
        return value.transpose(1, 0, 2).reshape(length, width).astype(BF)

    grad_qkv = jnp.concatenate([join(grad_q), join(grad_k), join(grad_v)], axis=1)
    grad_attn_w = mm_tn(h1, grad_qkv).astype(BF)
    attn_sum = lax.psum_scatter(grad_attn_w, "seq", scatter_dimension=0, tiled=True)
    grad_h1 = scatter_sum(grad_qkv, attn_mine, mm_nt)
    normed_own, scale_own = normalize(x_own)
    tokens_grad = (grad_middle + norm_back(grad_h1, gain_one, normed_own, scale_own)).astype(BF)

    mine_cols = jnp.arange(attn_cols, dtype=jnp.int32) + me * attn_cols
    attn_own = jnp.zeros((attn_sum.shape[0], attn_cols), F32)
    lanes = jnp.arange(width, dtype=jnp.int32)
    for b, block in zip(order, gather_blocks(attn_sum)):
        theirs = lanes + (me ^ b) * width
        theirs = jnp.concatenate([jnp.where(theirs < D, theirs + part * D, -1) for part in range(3)])
        attn_own = attn_own + mm(block, (theirs[:, None] == mine_cols[None, :]).astype(BF))
    fc_own = hidden_backward(fc_sum, unit).astype(F32)
    out_cols = w_fc2.shape[1]
    out_sent = jnp.stack([out_sum[:, c * out_cols : (c + 1) * out_cols] for c in range(count)])
    out_own = jnp.concatenate(exchange(out_sent), axis=0).astype(F32)

    def head_slots(value):
        return lax.dynamic_update_slice_in_dim(jnp.zeros((count * width,), F32), value, me * width, 0)[:D]

    sums = jnp.sum(grad_qkv.astype(F32), axis=0)
    grad_first = jnp.concatenate(
        [
            jnp.sum(grad_h1 * normed_own, axis=0),
            jnp.sum(grad_h1, axis=0),
            head_slots(sums[:width]),
            head_slots(sums[2 * width :]),
        ]
    )
    bf_sum = jnp.sum(grad_inner.astype(F32), axis=0).reshape(seqs, 1, unit)
    bf_slots = lax.dynamic_update_slice_in_dim(jnp.zeros((seqs, count, unit), F32), bf_sum, me, 1).reshape(-1)
    grad_second = jnp.concatenate(
        [
            jnp.sum(grad_middle, axis=0),
            jnp.sum(grad_h2 * normed_two, axis=0),
            jnp.sum(grad_h2, axis=0),
            jnp.sum(dy_own, axis=0),
            bf_slots,
        ]
    )
    first_own = lax.psum_scatter(grad_first, ("seq", "ctx"), scatter_dimension=0, tiled=True)
    second_own = lax.psum_scatter(grad_second, ("seq", "ctx"), scatter_dimension=0, tiled=True)
    return (output[None], tokens_grad[None], attn_own, proj_own, fc_own, out_own, first_own, second_own)


def solution(mesh):
    rows = P("seq", "ctx", None)
    weight = P("seq", "ctx")
    vector = P(("seq", "ctx"))
    return jax.shard_map(
        body,
        mesh=mesh,
        in_specs=(rows, rows, P("seq", None), P(), weight, weight, weight, weight, vector, vector),
        out_specs=(rows, rows, weight, weight, weight, weight, vector, vector),
        check_vma=False,
    )
```

```python
import jax
import jax.numpy as jnp
from jax import lax
from jax.sharding import PartitionSpec as P

D = 1600
FF = 6400
H = 25
HD = 64
BF = jnp.bfloat16
F32 = jnp.float32


def mm(a, b):
    return jnp.dot(a, b, preferred_element_type=F32)


def mm_nt(a, b):
    return lax.dot_general(a, b, (((1,), (1,)), ((), ())), preferred_element_type=F32)


def mm_tn(a, b):
    return lax.dot_general(a, b, (((0,), (0,)), ((), ())), preferred_element_type=F32)


def swap(value, step):
    count = lax.axis_size("ctx")
    return lax.ppermute(value, "ctx", [(i, i ^ step) for i in range(count)])


def swap_seq(value, step):
    seqs = lax.axis_size("seq")
    return lax.ppermute(value, "seq", [(i, i ^ step) for i in range(seqs)])


def local_order(count):
    return list(range(0, count, 2)) + list(range(1, count, 2))


def gather_blocks(own):
    count = lax.axis_size("ctx")
    even = [own] + [swap(own, step) for step in range(2, count, 2)]
    odd = [swap(block, 1) for block in even]
    return even + odd


def gather_rows(own):
    return jnp.concatenate(gather_blocks(own), axis=0)


def scatter_sum(left, right_weight, product):
    count = lax.axis_size("ctx")
    half = left.shape[0] // 2
    rows = left.shape[0] // count
    other = product(left[half:], right_weight).astype(BF)
    mine = product(left[:half], right_weight)
    mine = mine + swap(other, 1).astype(F32)
    total = mine[:rows]
    for number in range(1, count // 2):
        block = mine[number * rows : (number + 1) * rows].astype(BF)
        total = total + swap(block, 2 * number).astype(F32)
    return total


def pick(stack, number):
    return lax.dynamic_index_in_dim(stack, number, 0, keepdims=False)


def exchange(blocks_by_owner):
    count = lax.axis_size("ctx")
    me = lax.axis_index("ctx")
    got = jnp.stack([swap(pick(blocks_by_owner, me ^ step), step) if step else pick(blocks_by_owner, me) for step in range(count)])
    return [pick(got, me ^ sender) for sender in range(count)]


def seq_gather(part):
    return lax.all_gather(part, "seq", axis=0, tiled=True)


def seq_scatter(whole):
    seqs = lax.axis_size("seq")
    return lax.psum_scatter(whole.reshape(seqs, -1, whole.shape[1]), "seq", scatter_dimension=0, tiled=False)


def gather_vectors(part):
    seqs, count = lax.axis_size("seq"), lax.axis_size("ctx")
    me, row = lax.axis_index("ctx"), lax.axis_index("seq")
    size = part.shape[0]
    part = jnp.pad(part, (0, -size % 128)).reshape(-1, 128)
    got = jnp.stack([part] + [swap_seq(part, step) for step in range(1, seqs)])
    got = jnp.stack([pick(got, row ^ sender) for sender in range(seqs)])
    blocks = gather_blocks(got)
    by_step = [block for _, block in sorted(zip(local_order(count), blocks), key=lambda pair: pair[0])]
    by_step = jnp.stack(by_step)
    whole = jnp.stack([pick(by_step, me ^ sender) for sender in range(count)])
    return whole.transpose(1, 0, 2, 3).reshape(seqs, count, -1)[:, :, :size]


def scatter_vectors(whole):
    seqs, count = lax.axis_size("seq"), lax.axis_size("ctx")
    me, row = lax.axis_index("ctx"), lax.axis_index("seq")
    size = whole.shape[2]
    whole = jnp.pad(whole, ((0, 0), (0, 0), (0, -size % 128))).transpose(1, 0, 2)
    mine = pick(whole, me)
    for step in range(1, count):
        mine = mine + swap(pick(whole, me ^ step), step)
    mine = mine.reshape(seqs, -1, 128)
    own = pick(mine, row)
    for step in range(1, seqs):
        own = own + swap_seq(pick(mine, row ^ step), step)
    return own.reshape(-1)[:size]


def hidden_forward(w_fc, unit):
    seqs, count = lax.axis_size("seq"), lax.axis_size("ctx")
    assert count == 2 * seqs
    me = lax.axis_index("ctx")
    stack = jnp.stack([w_fc[:, k * unit : (k + 1) * unit] for k in range(seqs)])
    got = []
    for step in range(seqs):
        pairs = [(2 * (v ^ step) + u, seqs * u + v) for u in range(2) for v in range(seqs)]
        got.append(lax.ppermute(pick(stack, (me // 2) ^ step), "ctx", pairs))
    got = jnp.stack(got)
    return jnp.concatenate([pick(got, (me % seqs) ^ k) for k in range(seqs)], axis=1)


def hidden_backward(grad, unit):
    seqs = lax.axis_size("seq")
    me = lax.axis_index("ctx")
    stack = jnp.stack([grad[:, k * unit : (k + 1) * unit] for k in range(seqs)])
    got = []
    for step in range(seqs):
        pairs = [(seqs * u + v, 2 * (v ^ step) + u) for u in range(2) for v in range(seqs)]
        got.append(lax.ppermute(pick(stack, (me % seqs) ^ step), "ctx", pairs))
    got = jnp.stack(got)
    return jnp.concatenate([pick(got, (me // 2) ^ k) for k in range(seqs)], axis=1)


def gelu_and_grad(a):
    inner = 0.7978845608028654 * (a + 0.044715 * a * a * a)
    t = jnp.tanh(inner)
    value = 0.5 * a * (1.0 + t)
    slope = 0.5 * (1.0 + t) + 0.5 * a * (1.0 - t * t) * 0.7978845608028654 * (1.0 + 3 * 0.044715 * a * a)
    return value, slope


def normalize(values):
    average = jnp.mean(values, axis=-1, keepdims=True)
    centred = values - average
    scale = lax.rsqrt(jnp.mean(centred * centred, axis=-1, keepdims=True) + 1e-05)
    return centred * scale, scale


def norm_back(grad, gain, normed, scale):
    e = grad * gain
    return scale * (
        e - jnp.mean(e, axis=-1, keepdims=True) - normed * jnp.mean(e * normed, axis=-1, keepdims=True)
    )


def body(tokens, cotangent, segments, block_order, w_attn, w_proj, w_fc, w_fc2, attn_vectors, other_vectors):
    seqs, count = lax.axis_size("seq"), lax.axis_size("ctx")
    me = lax.axis_index("ctx")
    rows = tokens.shape[1]
    length = rows * count
    half_block = rows // 2
    heads = -(-H // count)
    width = heads * HD
    unit = FF // (seqs * count)
    order = local_order(count)

    attn_cols = w_attn.shape[1]
    attn_blocks = gather_blocks(w_attn)
    wanted = jnp.arange(width, dtype=jnp.int32) + me * width
    wanted = jnp.concatenate([jnp.where(wanted < D, wanted + part * D, -1) for part in range(3)])

    def chosen(owner):
        return (jnp.arange(attn_cols, dtype=jnp.int32)[:, None] + owner * attn_cols) == wanted[None, :]

    attn_part = sum(mm(block, chosen(me ^ b).astype(BF)) for b, block in zip(order, attn_blocks)).astype(BF)
    proj_cols = w_proj.shape[1]
    proj_all = seq_gather(w_proj)
    attn_mine = seq_gather(attn_part)
    fc_mine = seq_gather(hidden_forward(w_fc, unit))
    out_blocks = exchange(w_fc2.reshape(count, unit, w_fc2.shape[1]))
    out_mine = seq_gather(jnp.concatenate(out_blocks, axis=1))
    proj_pad = jnp.pad(proj_all, ((0, count * width - D), (0, 0))).reshape(count, width, proj_cols)
    proj_mine = jnp.concatenate(exchange(proj_pad), axis=1)

    vectors = gather_vectors(jnp.concatenate([attn_vectors, other_vectors]))
    first_all = vectors[:, :, : attn_vectors.shape[0]].reshape(-1).astype(F32)
    second_all = vectors[:, :, attn_vectors.shape[0] :].reshape(-1).astype(F32)
    gain_one, shift_one, bias_query, bias_value = [first_all[n * D : (n + 1) * D] for n in range(4)]
    bias_proj, gain_two, shift_two, bias_out = [second_all[n * D : (n + 1) * D] for n in range(4)]
    bias_fc = pick(second_all[4 * D :].reshape(seqs, count, unit).transpose(1, 0, 2), me).reshape(-1)

    def my_heads(vector):
        return lax.dynamic_slice_in_dim(jnp.pad(vector, (0, count * width - D)), me * width, width)

    x_own = tokens[0].astype(F32)
    x_all = gather_rows(tokens[0]).astype(F32)
    normed_one, _ = normalize(x_all)
    h1 = (normed_one * gain_one + shift_one).astype(BF)
    bias_joined = jnp.concatenate([my_heads(bias_query), jnp.zeros((width,), F32), my_heads(bias_value)])
    qkv = (mm(h1, attn_mine) + bias_joined).astype(BF)

    owners = jnp.stack([me ^ b for b in order])
    stored = (owners[:, None] * 2 + jnp.arange(2, dtype=jnp.int32)[None, :]).reshape(-1)
    blocks = jnp.take(block_order, stored)
    places = (blocks[:, None] * half_block + jnp.arange(half_block, dtype=jnp.int32)[None, :]).reshape(-1)
    labels = jnp.take(segments[0].reshape(-1, half_block), blocks, axis=0).reshape(-1)
    allowed = (places[None, :] <= places[:, None]) & (labels[None, :] == labels[:, None])

    def split(value):
        return value.reshape(length, heads, HD).transpose(1, 0, 2)

    q = split(qkv[:, :width]) * BF(0.125)
    k = split(qkv[:, width : 2 * width])
    v = split(qkv[:, 2 * width :])
    scores = jnp.einsum("hqd,hkd->hqk", q, k, preferred_element_type=F32)
    scores = jnp.where(allowed[None], scores, -1e30)
    highest = jnp.max(scores, axis=-1, keepdims=True)
    weights = jnp.exp(scores - highest)
    total = jnp.sum(weights, axis=-1, keepdims=True)
    lse = highest + jnp.log(total)
    mixed = jnp.einsum("hqk,hkd->hqd", weights.astype(BF), v, preferred_element_type=F32) / total
    attended = mixed.transpose(1, 0, 2).reshape(length, width).astype(BF)
    middle = x_own + scatter_sum(attended, proj_mine, mm) + bias_proj
    normed_two, scale_two = normalize(middle)
    h2 = gather_rows((normed_two * gain_two + shift_two).astype(BF))
    inner = mm(h2, fc_mine) + bias_fc
    active, slope = gelu_and_grad(inner)
    active = active.astype(BF)
    output = (middle + scatter_sum(active, out_mine, mm) + bias_out).astype(BF)

    dy_own = cotangent[0].astype(F32)
    dy = gather_rows(cotangent[0])
    grad_inner = (mm_nt(dy, out_mine) * slope).astype(BF)
    grad_out_w = mm_tn(active, dy).astype(BF)
    grad_fc_w = mm_tn(h2, grad_inner).astype(BF)
    out_sum = seq_scatter(grad_out_w)
    fc_sum = seq_scatter(grad_fc_w)
    grad_h2 = scatter_sum(grad_inner, fc_mine, mm_nt)
    grad_middle = dy_own + norm_back(grad_h2, gain_two, normed_two, scale_two)
    r_all = gather_rows(grad_middle.astype(BF))
    grad_proj_w = mm_tn(attended, r_all).astype(BF)
    proj_sent = jnp.stack([grad_proj_w[:, c * proj_cols : (c + 1) * proj_cols] for c in range(count)])
    proj_part = jnp.concatenate(exchange(proj_sent), axis=0)[:D]
    proj_own = seq_scatter(proj_part).astype(F32)

    grad_heads = split(mm_nt(r_all, proj_mine).astype(BF))
    prob = jnp.exp(scores - lse)
    grad_v = jnp.einsum("hqk,hqd->hkd", prob.astype(BF), grad_heads, preferred_element_type=F32)
    grad_prob = jnp.einsum("hqd,hkd->hqk", grad_heads, v, preferred_element_type=F32)
    delta = jnp.sum(grad_heads.astype(F32) * mixed, axis=-1, keepdims=True)
    grad_scores = (prob * (grad_prob - delta)).astype(BF)
    grad_q = jnp.einsum("hqk,hkd->hqd", grad_scores, k, preferred_element_type=F32) * 0.125
    grad_k = jnp.einsum("hqk,hqd->hkd", grad_scores, q, preferred_element_type=F32)

    def join(value):
        return value.transpose(1, 0, 2).reshape(length, width).astype(BF)

    grad_qkv = jnp.concatenate([join(grad_q), join(grad_k), join(grad_v)], axis=1)
    grad_attn_w = mm_tn(h1, grad_qkv).astype(BF)
    attn_sum = seq_scatter(grad_attn_w)
    grad_h1 = scatter_sum(grad_qkv, attn_mine, mm_nt)
    normed_own, scale_own = normalize(x_own)
    tokens_grad = (grad_middle + norm_back(grad_h1, gain_one, normed_own, scale_own)).astype(BF)

    mine_cols = jnp.arange(attn_cols, dtype=jnp.int32) + me * attn_cols
    attn_own = jnp.zeros((attn_sum.shape[0], attn_cols), F32)
    lanes = jnp.arange(width, dtype=jnp.int32)
    for b, block in zip(order, gather_blocks(attn_sum)):
        theirs = lanes + (me ^ b) * width
        theirs = jnp.concatenate([jnp.where(theirs < D, theirs + part * D, -1) for part in range(3)])
        attn_own = attn_own + mm(block, (theirs[:, None] == mine_cols[None, :]).astype(BF))
    fc_own = hidden_backward(fc_sum, unit).astype(F32)
    out_cols = w_fc2.shape[1]
    out_sent = jnp.stack([out_sum[:, c * out_cols : (c + 1) * out_cols] for c in range(count)])
    out_own = jnp.concatenate(exchange(out_sent), axis=0).astype(F32)

    def head_slots(value):
        return lax.dynamic_update_slice_in_dim(jnp.zeros((count * width,), F32), value, me * width, 0)[:D]

    sums = jnp.sum(grad_qkv.astype(F32), axis=0)
    grad_first = jnp.concatenate(
        [
            jnp.sum(grad_h1 * normed_own, axis=0),
            jnp.sum(grad_h1, axis=0),
            head_slots(sums[:width]),
            head_slots(sums[2 * width :]),
        ]
    )
    bf_sum = jnp.sum(grad_inner.astype(F32), axis=0).reshape(seqs, 1, unit)
    bf_slots = lax.dynamic_update_slice_in_dim(jnp.zeros((seqs, count, unit), F32), bf_sum, me, 1).reshape(-1)
    grad_second = jnp.concatenate(
        [
            jnp.sum(grad_middle, axis=0),
            jnp.sum(grad_h2 * normed_two, axis=0),
            jnp.sum(grad_h2, axis=0),
            jnp.sum(dy_own, axis=0),
            bf_slots,
        ]
    )
    first_own = scatter_vectors(grad_first.reshape(seqs, count, -1))
    second_own = scatter_vectors(grad_second.reshape(seqs, count, -1))
    return (output[None], tokens_grad[None], attn_own, proj_own, fc_own, out_own, first_own, second_own)


def solution(mesh):
    rows = P("seq", "ctx", None)
    weight = P("seq", "ctx")
    vector = P(("seq", "ctx"))
    return jax.shard_map(
        body,
        mesh=mesh,
        in_specs=(rows, rows, P("seq", None), P(), weight, weight, weight, weight, vector, vector),
        out_specs=(rows, rows, weight, weight, weight, weight, vector, vector),
        check_vma=False,
    )
```

```python
import jax
import jax.numpy as jnp
from jax import lax
from jax.experimental import pallas as pl
from jax.experimental.layout import Layout, with_layout_constraint
from jax.experimental.pallas import tpu as pltpu
from jax.sharding import PartitionSpec as P

D = 1600
FF = 6400
H = 25
HD = 64
BF = jnp.bfloat16
F32 = jnp.float32


def mm(a, b):
    return jnp.dot(a, b, preferred_element_type=F32)


def mm_nt(a, b):
    return lax.dot_general(a, b, (((1,), (1,)), ((), ())), preferred_element_type=F32)


def mm_tn(a, b):
    return lax.dot_general(a, b, (((0,), (0,)), ((), ())), preferred_element_type=F32)


def swap(value, step):
    count = lax.axis_size("ctx")
    return lax.ppermute(value, "ctx", [(i, i ^ step) for i in range(count)])


def swap_seq(value, step):
    seqs = lax.axis_size("seq")
    return lax.ppermute(value, "seq", [(i, i ^ step) for i in range(seqs)])


def local_order(count):
    return list(range(0, count, 2)) + list(range(1, count, 2))


def after(value, *others):
    return lax.optimization_barrier((value, *others))[0]


def pick(stack, number, axis=0):
    return lax.dynamic_index_in_dim(stack, number, axis, keepdims=False)


def gather_blocks(own):
    count = lax.axis_size("ctx")
    even = [own] + [swap(own, step) for step in range(2, count, 2)]
    odd = [swap(block, 1) for block in even]
    return even, odd


def gather_rows(own):
    count = lax.axis_size("ctx")
    mine = jnp.concatenate([own] + [swap(own, step) for step in range(2, count, 2)], axis=0)
    return mine, swap(mine, 1)


def scatter_sum(left, product, fillers=()):
    count = lax.axis_size("ctx")
    rows = left[0].shape[0] * 2 // count
    other = product(left[1]).astype(BF)
    mine = product(left[0])
    mine = mine + swap(other, 1).astype(F32)
    blocks = [mine[number * rows : (number + 1) * rows].astype(BF) for number in range(1, count // 2)]
    blocks = [swap(block, 2 * number) for number, block in enumerate(blocks, 1)]
    if fillers:
        blocks, fillers = lax.optimization_barrier((blocks, fillers))
    total = mine[:rows]
    for block in blocks:
        total = total + block.astype(F32)
    return (total, fillers) if fillers else total


def both(function, *halves):
    return tuple(function(*pair) for pair in zip(*halves))


def over_rows(left, right):
    return mm_tn(left[0], right[0]) + mm_tn(left[1], right[1])


VMEM_LIMIT = 56 * 1024 * 1024


def small_kernel(kernel, shape, key, *arrays, scratch=()):
    return pl.pallas_call(
        kernel,
        out_shape=shape,
        in_specs=[pl.BlockSpec(memory_space=pltpu.SMEM)] + [pl.BlockSpec(memory_space=pltpu.VMEM)] * len(arrays),
        out_specs=pl.BlockSpec(memory_space=pltpu.VMEM),
        scratch_shapes=list(scratch),
    )(key.reshape(1), *arrays)


def split_columns(whole, number, key):
    rows, width = whole.shape[0], whole.shape[1] // number

    def kernel(key_ref, whole_ref, out_ref):
        for k in range(number):
            out_ref[k ^ key_ref[0]] = whole_ref[:, k * width : (k + 1) * width]

    return small_kernel(kernel, jax.ShapeDtypeStruct((number, rows, width), whole.dtype), key, whole)


def split_rows(whole, number, key):
    stack = whole.reshape(number, -1, whole.shape[1])

    def kernel(key_ref, stack_ref, out_ref):
        for k in range(number):
            out_ref[k ^ key_ref[0]] = stack_ref[k]

    return small_kernel(kernel, jax.ShapeDtypeStruct(stack.shape, whole.dtype), key, stack)


def join(parts, key, axis, dtype=None):
    dtype = dtype or parts[0].dtype
    number = sum(part.shape[0] for part in parts)
    rows, width = parts[0].shape[1:]
    shape = (rows, number * width) if axis == 1 else (number * rows, width)

    def kernel(key_ref, *refs):
        out_ref, stack = refs[-2:]
        at = 0
        for ref in refs[:-2]:
            for n in range(ref.shape[0]):
                stack[at] = ref[n]
                at += 1
        for k in range(number):
            part = stack[k ^ key_ref[0]].astype(dtype)
            if axis == 1:
                out_ref[:, k * width : (k + 1) * width] = part
            else:
                out_ref[k * rows : (k + 1) * rows, :] = part

    stack = pltpu.VMEM((number, rows, width), parts[0].dtype)
    return small_kernel(kernel, jax.ShapeDtypeStruct(shape, dtype), key, *parts, scratch=[stack])


def exchange(stack):
    count = lax.axis_size("ctx")
    pairs = stack.reshape(count // 2, 2, *stack.shape[1:])
    came = swap(pairs[:, 1], 1)
    sent = jnp.stack([pairs[:, 0], came], axis=1)
    return [sent[0]] + [swap(sent[step], 2 * step) for step in range(1, count // 2)]


def attention_forward(qkv, places, labels, heads):
    width, length = qkv.shape[0] // 3, qkv.shape[1]
    block = min(256, length)

    def kernel(pc_ref, lc_ref, pr_ref, lr_ref, q_ref, k_ref, v_ref, o_ref, low_ref, lse_ref, bias, keys):
        head, part = pl.program_id(0), pl.program_id(1)
        cols = pl.ds(pl.multiple_of(part * block, block), block)

        @pl.when(head == 0)
        def _():
            allowed = (pc_ref[...] <= pr_ref[:, cols]) & (lc_ref[...] == lr_ref[:, cols])
            bias[:, cols] = jnp.where(allowed, 0.0, -1e30)

        @pl.when(part == 0)
        def _():
            keys[...] = k_ref[...].T

        query = q_ref[:, cols] * BF(0.125)
        scores = mm(keys[...], query) + bias[:, cols]
        highest = jnp.max(scores, axis=0, keepdims=True)
        weights = jnp.exp(scores - highest)
        total = jnp.sum(weights, axis=0, keepdims=True)
        mixed = mm(v_ref[...], weights.astype(BF)) / total
        o_ref[:, cols] = mixed
        low_ref[:, cols] = mixed.astype(BF)
        lse_ref[0, :, cols] = highest + jnp.log(total)

    def full(shape):
        return pl.BlockSpec(shape, lambda h, p: (0,) * len(shape))

    def head_rows(offset):
        return pl.BlockSpec((HD, length), lambda h, p: (h + offset, 0))

    return pl.pallas_call(
        kernel,
        grid=(heads, length // block),
        out_shape=(
            jax.ShapeDtypeStruct((width, length), F32),
            jax.ShapeDtypeStruct((width, length), BF),
            jax.ShapeDtypeStruct((heads, 1, length), F32),
        ),
        in_specs=[full((length, 1))] * 2 + [full((1, length))] * 2 + [head_rows(0), head_rows(heads), head_rows(2 * heads)],
        out_specs=(head_rows(0), head_rows(0), pl.BlockSpec((1, 1, length), lambda h, p: (h, 0, 0))),
        scratch_shapes=[pltpu.VMEM((length, length), F32), pltpu.VMEM((length, HD), BF)],
        compiler_params=pltpu.CompilerParams(vmem_limit_bytes=VMEM_LIMIT),
        cost_estimate=pl.CostEstimate(
            flops=16 * heads * length * length * HD, bytes_accessed=12 * width * length, transcendentals=heads * length * length
        ),
    )(places[:, None], labels[:, None], places[None], labels[None], qkv, qkv, qkv)


def attention_backward(qkv, places, labels, mixed, lse, grad, heads):
    width, length = qkv.shape[0] // 3, qkv.shape[1]
    block = min(256, length)

    def kernel(pc_ref, lc_ref, pr_ref, lr_ref, q_ref, k_ref, v_ref, o_ref, lse_ref, g_ref, out_ref, bias, keys, values, dk, dv):
        head, part = pl.program_id(0), pl.program_id(1)
        cols = pl.ds(pl.multiple_of(part * block, block), block)

        @pl.when(head == 0)
        def _():
            allowed = (pc_ref[...] <= pr_ref[:, cols]) & (lc_ref[...] == lr_ref[:, cols])
            bias[:, cols] = jnp.where(allowed, 0.0, -1e30)

        @pl.when(part == 0)
        def _():
            keys[...] = k_ref[...].T
            values[...] = v_ref[...].T
            dk[...] = jnp.zeros_like(dk)
            dv[...] = jnp.zeros_like(dv)

        query = q_ref[:, cols] * BF(0.125)
        grads = g_ref[:, cols]
        delta = jnp.sum(grads.astype(F32) * o_ref[:, cols], axis=0, keepdims=True)
        scores = mm(keys[...], query) + bias[:, cols]
        prob = jnp.exp(scores - lse_ref[0, :, cols])
        prob_grad = mm(values[...], grads)
        score_grad = (prob * (prob_grad - delta)).astype(BF)
        dv[...] += mm_nt(grads, prob.astype(BF))
        dk[...] += mm_nt(query, score_grad)
        out_ref[0, :, cols] = (mm(k_ref[...], score_grad) * 0.125).astype(BF)

        @pl.when(part == pl.num_programs(1) - 1)
        def _():
            out_ref[1] = dk[...].astype(BF)
            out_ref[2] = dv[...].astype(BF)

    def full(shape):
        return pl.BlockSpec(shape, lambda h, p: (0,) * len(shape))

    def head_rows(offset):
        return pl.BlockSpec((HD, length), lambda h, p: (h + offset, 0))

    return pl.pallas_call(
        kernel,
        grid=(heads, length // block),
        out_shape=jax.ShapeDtypeStruct((3, width, length), BF),
        in_specs=[full((length, 1))] * 2
        + [full((1, length))] * 2
        + [head_rows(0), head_rows(heads), head_rows(2 * heads), head_rows(0)]
        + [pl.BlockSpec((1, 1, length), lambda h, p: (h, 0, 0)), head_rows(0)],
        out_specs=pl.BlockSpec((3, HD, length), lambda h, p: (0, h, 0)),
        scratch_shapes=[
            pltpu.VMEM((length, length), F32),
            pltpu.VMEM((length, HD), BF),
            pltpu.VMEM((length, HD), BF),
            pltpu.VMEM((HD, length), F32),
            pltpu.VMEM((HD, length), F32),
        ],
        compiler_params=pltpu.CompilerParams(vmem_limit_bytes=VMEM_LIMIT),
        cost_estimate=pl.CostEstimate(
            flops=40 * heads * length * length * HD, bytes_accessed=16 * width * length, transcendentals=heads * length * length
        ),
    )(places[:, None], labels[:, None], places[None], labels[None], qkv, qkv, qkv, mixed, lse, grad)


def seq_gather(part):
    return lax.all_gather(part, "seq", axis=0, tiled=True)


def seq_scatter(whole):
    seqs = lax.axis_size("seq")
    return lax.psum_scatter(whole.reshape(seqs, -1, whole.shape[1]), "seq", scatter_dimension=0, tiled=False)


def seq_gather_direct(part):
    seqs = lax.axis_size("seq")
    row = lax.axis_index("seq")
    got = jnp.stack([part] + [swap_seq(part, step) for step in range(1, seqs)])
    return jnp.concatenate([pick(got, row ^ sender) for sender in range(seqs)], axis=0)


def seq_scatter_direct(whole):
    seqs = lax.axis_size("seq")
    row = lax.axis_index("seq")
    stack = whole.reshape(seqs, -1, whole.shape[1])
    total = pick(stack, row).astype(F32)
    for step in range(1, seqs):
        total = total + swap_seq(pick(stack, row ^ step), step).astype(F32)
    return total


def everywhere(part):
    number = lax.axis_size("seq") * lax.axis_size("ctx")
    size = part.shape[0]
    part = jnp.pad(part, (0, -size % 128)).reshape(1, -1, 128)
    whole = jnp.broadcast_to(part, (number, *part.shape[1:]))
    whole = lax.all_to_all(whole, ("seq", "ctx"), split_axis=0, concat_axis=0, tiled=True)
    return whole.reshape(number, -1)[:, :size]


def sum_to_owner(whole):
    number, size = whole.shape
    whole = jnp.pad(whole, ((0, 0), (0, -size % 128))).reshape(number, -1, 128)
    whole = lax.all_to_all(whole, ("seq", "ctx"), split_axis=0, concat_axis=0, tiled=True)
    return jnp.sum(whole, axis=0).reshape(-1)[:size]


def hidden_pairs(step, seqs):
    return [(2 * (v ^ step) + u, seqs * u + v) for u in range(2) for v in range(seqs)]


def hidden_forward(w_fc):
    seqs, count = lax.axis_size("seq"), lax.axis_size("ctx")
    assert count == 2 * seqs
    me = lax.axis_index("ctx")
    sent = split_columns(w_fc, seqs, me // 2)
    got = [lax.ppermute(sent[step : step + 1], "ctx", hidden_pairs(step, seqs)) for step in range(seqs)]
    return join(got, me % seqs, 1)


def hidden_backward(grad):
    seqs = lax.axis_size("seq")
    me = lax.axis_index("ctx")
    sent = split_columns(grad, seqs, me % seqs)
    got = [
        lax.ppermute(sent[step : step + 1], "ctx", [(d, c) for c, d in hidden_pairs(step, seqs)]) for step in range(seqs)
    ]
    return join(got, me // 2, 1, F32)


def gelu_and_grad(a):
    inner = 0.7978845608028654 * (a + 0.044715 * a * a * a)
    t = jnp.tanh(inner)
    value = 0.5 * a * (1.0 + t)
    slope = 0.5 * (1.0 + t) + 0.5 * a * (1.0 - t * t) * 0.7978845608028654 * (1.0 + 3 * 0.044715 * a * a)
    return value, slope


def normalize(values):
    average = jnp.mean(values, axis=-1, keepdims=True)
    centred = values - average
    scale = lax.rsqrt(jnp.mean(centred * centred, axis=-1, keepdims=True) + 1e-05)
    return centred * scale, scale


def norm_back(grad, gain, normed, scale):
    e = grad * gain
    return scale * (
        e - jnp.mean(e, axis=-1, keepdims=True) - normed * jnp.mean(e * normed, axis=-1, keepdims=True)
    )


def body(tokens, cotangent, segments, block_order, w_attn, w_proj, w_fc, w_fc2, attn_vectors, other_vectors):
    seqs, count = lax.axis_size("seq"), lax.axis_size("ctx")
    me = lax.axis_index("ctx")
    rows = tokens.shape[1]
    length = rows * count
    half_block = rows // 2
    heads = -(-H // count)
    width = heads * HD
    unit = FF // (seqs * count)
    order = local_order(count)

    attn_cols = w_attn.shape[1]
    attn_even, attn_odd = gather_blocks(w_attn)
    wanted = jnp.arange(width, dtype=jnp.int32) + me * width
    wanted = jnp.concatenate([jnp.where(wanted < D, wanted + part * D, -1) for part in range(3)])

    def chosen(owner):
        return (jnp.arange(attn_cols, dtype=jnp.int32)[:, None] + owner * attn_cols) == wanted[None, :]

    attn_part = sum(mm(block, chosen(me ^ b).astype(BF)) for b, block in zip(order, attn_even + attn_odd)).astype(BF)
    attn_mine = seq_gather(attn_part)
    vectors = everywhere(jnp.concatenate([attn_vectors, other_vectors]))
    proj_cols = w_proj.shape[1]
    proj_all = seq_gather_direct(w_proj)
    x_all = gather_rows(after(tokens[0], attn_even))
    fc_start, out_start, proj_all = lax.optimization_barrier((w_fc, w_fc2, proj_all, x_all[0]))[:3]
    fc_mine = seq_gather(hidden_forward(fc_start))
    out_part = join(exchange(split_rows(out_start, count, me)), me, 1)
    out_mine = seq_gather(out_part)
    proj_pad = jnp.pad(proj_all, ((0, count * width - D), (0, 0)))
    proj_mine = join(exchange(split_rows(proj_pad, count, me)), me, 1)

    first_all = vectors[:, : attn_vectors.shape[0]].reshape(-1).astype(F32)
    second_all = vectors[:, attn_vectors.shape[0] :].reshape(-1).astype(F32)
    gain_one, shift_one, bias_query, bias_value = [first_all[n * D : (n + 1) * D] for n in range(4)]
    bias_proj, gain_two, shift_two, bias_out = [second_all[n * D : (n + 1) * D] for n in range(4)]
    bias_fc = pick(second_all[4 * D :].reshape(seqs, count, unit).transpose(1, 0, 2), me).reshape(-1)

    def my_heads(vector):
        return lax.dynamic_slice_in_dim(jnp.pad(vector, (0, count * width - D)), me * width, width)

    x_own = tokens[0].astype(F32)
    h1 = both(lambda x: (normalize(x.astype(F32))[0] * gain_one + shift_one).astype(BF), x_all)
    bias_joined = jnp.concatenate([my_heads(bias_query), jnp.zeros((width,), F32), my_heads(bias_value)])
    qkv = jnp.concatenate([(mm(h, attn_mine) + bias_joined).astype(BF) for h in h1], axis=0).T

    owners = jnp.stack([me ^ b for b in order])
    stored = (owners[:, None] * 2 + jnp.arange(2, dtype=jnp.int32)[None, :]).reshape(-1)
    blocks = jnp.take(block_order, stored)
    places = (blocks[:, None] * half_block + jnp.arange(half_block, dtype=jnp.int32)[None, :]).reshape(-1)
    labels = jnp.take(segments[0].reshape(-1, half_block), blocks, axis=0).reshape(-1)
    mixed, attended, lse = attention_forward(qkv, places, labels, heads)
    half = length // 2
    attended = (attended[:, :half].T, attended[:, half:].T)
    middle = x_own + scatter_sum(attended, lambda o: mm(o, proj_mine)) + bias_proj
    normed_two, scale_two = normalize(middle)
    h2 = gather_rows((normed_two * gain_two + shift_two).astype(BF))
    active, slope = zip(*[gelu_and_grad(mm(h, fc_mine) + bias_fc) for h in h2])
    active = both(lambda g: g.astype(BF), active)

    dy_own = cotangent[0].astype(F32)
    dy = gather_rows(after(cotangent[0], qkv))
    grad_inner = both(lambda g, d: (mm_nt(g, out_mine) * d).astype(BF), dy, slope)
    grad_out_w = over_rows(active, dy).astype(BF)
    grad_fc_w = over_rows(h2, grad_inner).astype(BF)
    fillers = tuple(with_layout_constraint(g, Layout((0, 1))) for g in (grad_out_w, grad_fc_w))
    grad_h2, (grad_out_w, grad_fc_w) = scatter_sum(grad_inner, lambda d: mm_nt(d, fc_mine), fillers)
    out_sum = seq_scatter(grad_out_w)
    fc_sum = seq_scatter(grad_fc_w)
    grad_middle = dy_own + norm_back(grad_h2, gain_two, normed_two, scale_two)
    r_all = gather_rows(grad_middle.astype(BF))
    output = (middle + scatter_sum(after(active, r_all[0]), lambda g: mm(g, out_mine)) + bias_out).astype(BF)
    grad_proj_w = over_rows(attended, r_all).astype(BF)
    proj_part = join(exchange(split_columns(grad_proj_w, count, me)), me, 0)[:D]
    proj_own = seq_scatter_direct(proj_part)

    grad_mixed = jnp.concatenate([mm_nt(r, proj_mine).astype(BF) for r in r_all], axis=0).T
    grad_qkv = attention_backward(qkv, places, labels, mixed, lse, grad_mixed, heads).reshape(3 * width, length)
    sums = jnp.sum(grad_qkv.astype(F32), axis=1)
    grad_qkv = (grad_qkv[:, :half].T, grad_qkv[:, half:].T)
    grad_attn_w = over_rows(h1, grad_qkv).astype(BF)
    attn_sum = seq_scatter(grad_attn_w)
    grad_h1 = scatter_sum(grad_qkv, lambda d: mm_nt(d, attn_mine))
    normed_own, scale_own = normalize(x_own)
    tokens_grad = (grad_middle + norm_back(grad_h1, gain_one, normed_own, scale_own)).astype(BF)

    mine_cols = jnp.arange(attn_cols, dtype=jnp.int32) + me * attn_cols
    attn_own = jnp.zeros((attn_sum.shape[0], attn_cols), F32)
    lanes = jnp.arange(width, dtype=jnp.int32)
    for b, block in zip(order, sum(gather_blocks(attn_sum), [])):
        theirs = lanes + (me ^ b) * width
        theirs = jnp.concatenate([jnp.where(theirs < D, theirs + part * D, -1) for part in range(3)])
        attn_own = attn_own + mm(block, (theirs[:, None] == mine_cols[None, :]).astype(BF))
    fc_own = hidden_backward(fc_sum)
    out_own = join(exchange(split_columns(out_sum, count, me)), me, 0, F32)

    def head_slots(value):
        return lax.dynamic_update_slice_in_dim(jnp.zeros((count * width,), F32), value, me * width, 0)[:D]

    grad_first = jnp.concatenate(
        [
            jnp.sum(grad_h1 * normed_own, axis=0),
            jnp.sum(grad_h1, axis=0),
            head_slots(sums[:width]),
            head_slots(sums[2 * width :]),
        ]
    )
    bf_sum = sum(jnp.sum(d.astype(F32), axis=0) for d in grad_inner).reshape(seqs, 1, unit)
    bf_slots = lax.dynamic_update_slice_in_dim(jnp.zeros((seqs, count, unit), F32), bf_sum, me, 1).reshape(-1)
    grad_second = jnp.concatenate(
        [
            jnp.sum(grad_middle, axis=0),
            jnp.sum(grad_h2 * normed_two, axis=0),
            jnp.sum(grad_h2, axis=0),
            jnp.sum(dy_own, axis=0),
            bf_slots,
        ]
    )
    number = seqs * count
    own = sum_to_owner(jnp.concatenate([grad_first.reshape(number, -1), grad_second.reshape(number, -1)], axis=1))
    first_own, second_own = own[: attn_vectors.shape[0]], own[attn_vectors.shape[0] :]
    return (output[None], tokens_grad[None], attn_own, proj_own, fc_own, out_own, first_own, second_own)


def solution(mesh):
    rows = P("seq", "ctx", None)
    weight = P("seq", "ctx")
    vector = P(("seq", "ctx"))
    return jax.shard_map(
        body,
        mesh=mesh,
        in_specs=(rows, rows, P("seq", None), P(), weight, weight, weight, weight, vector, vector),
        out_specs=(rows, rows, weight, weight, weight, weight, vector, vector),
        check_vma=False,
    )
```

```python
import jax
import jax.numpy as jnp
from jax import lax
from jax.experimental import pallas as pl
from jax.experimental.layout import Layout, with_layout_constraint
from jax.experimental.pallas import tpu as pltpu
from jax.sharding import PartitionSpec as P

D = 1600
FF = 6400
H = 25
HD = 64
BF = jnp.bfloat16
F32 = jnp.float32


def mm(a, b):
    return jnp.dot(a, b, preferred_element_type=F32)


def mm_nt(a, b):
    return lax.dot_general(a, b, (((1,), (1,)), ((), ())), preferred_element_type=F32)


def mm_tn(a, b):
    return lax.dot_general(a, b, (((0,), (0,)), ((), ())), preferred_element_type=F32)


def swap(value, step):
    count = lax.axis_size("ctx")
    return lax.ppermute(value, "ctx", [(i, i ^ step) for i in range(count)])


def swap_seq(value, step):
    seqs = lax.axis_size("seq")
    return lax.ppermute(value, "seq", [(i, i ^ step) for i in range(seqs)])


def local_order(count):
    return list(range(0, count, 2)) + list(range(1, count, 2))


def after(value, *others):
    return lax.optimization_barrier((value, *others))[0]


def pick(stack, number, axis=0):
    return lax.dynamic_index_in_dim(stack, number, axis, keepdims=False)


def gather_blocks(own):
    count = lax.axis_size("ctx")
    even = [own] + [swap(own, step) for step in range(2, count, 2)]
    odd = [swap(block, 1) for block in even]
    return even, odd


def gather_start(own):
    count = lax.axis_size("ctx")
    return [own] + [swap(own, step) for step in range(2, count, 2)]


def gather_finish(blocks):
    mine = jnp.concatenate(blocks, axis=0)
    return mine, swap(mine, 1)


def gather_rows(own):
    return gather_finish(gather_start(own))


def scatter_start(left, product):
    count = lax.axis_size("ctx")
    rows = left[0].shape[0] * 2 // count
    other = product(left[1]).astype(BF)
    mine = product(left[0])
    mine = mine + swap(other, 1).astype(F32)
    sent = [mine[number * rows : (number + 1) * rows].astype(BF) for number in range(1, count // 2)]
    return mine[:rows], sent, [swap(block, 2 * number) for number, block in enumerate(sent, 1)]


def scatter_finish(total, blocks):
    for block in blocks:
        total = total + block.astype(F32)
    return total


def scatter_sum(left, product, fillers=()):
    total, _, blocks = scatter_start(left, product)
    return scatter_finish(total, after(blocks, fillers) if fillers else blocks)


def both(function, *halves):
    return tuple(function(*pair) for pair in zip(*halves))


def over_rows(left, right):
    return mm_tn(left[0], right[0]) + mm_tn(left[1], right[1])


VMEM_LIMIT = 56 * 1024 * 1024


def small_kernel(kernel, shape, key, *arrays, scratch=()):
    return pl.pallas_call(
        kernel,
        out_shape=shape,
        in_specs=[pl.BlockSpec(memory_space=pltpu.SMEM)] + [pl.BlockSpec(memory_space=pltpu.VMEM)] * len(arrays),
        out_specs=pl.BlockSpec(memory_space=pltpu.VMEM),
        scratch_shapes=list(scratch),
    )(key.reshape(1), *arrays)


def split_columns(whole, number, key):
    rows, width = whole.shape[0], whole.shape[1] // number

    def kernel(key_ref, whole_ref, out_ref):
        for k in range(number):
            out_ref[k ^ key_ref[0]] = whole_ref[:, k * width : (k + 1) * width]

    return small_kernel(kernel, jax.ShapeDtypeStruct((number, rows, width), whole.dtype), key, whole)


def join(parts, key, dtype=None):
    dtype = dtype or parts[0].dtype
    number = sum(part.shape[0] for part in parts)
    rows, width = parts[0].shape[1:]

    def kernel(key_ref, *refs):
        out_ref, stack = refs[-2:]
        at = 0
        for ref in refs[:-2]:
            for n in range(ref.shape[0]):
                stack[at] = ref[n]
                at += 1
        for k in range(number):
            out_ref[:, k * width : (k + 1) * width] = stack[k ^ key_ref[0]].astype(dtype)

    stack = pltpu.VMEM((number, rows, width), parts[0].dtype)
    return small_kernel(kernel, jax.ShapeDtypeStruct((rows, number * width), dtype), key, *parts, scratch=[stack])


def lanes(cols):
    return -(-cols // 128) * 128


def pack_first(out_stack, vector_parts, row):
    count, unit, cols = out_stack.shape
    seqs, extra = len(vector_parts), vector_parts[0].shape[0]

    def kernel(row_ref, stack_ref, *refs):
        parts, out_ref, held = refs[:-2], refs[-2], refs[-1]
        for step, part in enumerate(parts):
            held[step ^ row_ref[0]] = part[...]
        for d in range(count):
            out_ref[d, :unit, :cols] = stack_ref[d]
            for owner in range(seqs):
                out_ref[d, unit + owner * extra : unit + (owner + 1) * extra, :cols] = held[owner]

    shape = jax.ShapeDtypeStruct((count, unit + seqs * extra, lanes(cols)), BF)
    held = pltpu.VMEM((seqs, extra, cols), BF)
    return small_kernel(kernel, shape, row, out_stack, *vector_parts, scratch=[held])


def unpack_first(got, unit, cols, first_size, second_size):
    count, total, _ = got.shape
    seqs = lax.axis_size("seq")
    extra = (total - unit) // seqs

    def kernel(got_ref, out_ref, first_ref, second_ref):
        for d in range(count):
            out_ref[:, d * cols : (d + 1) * cols] = got_ref[d, :unit, :cols]
            for owner in range(seqs):
                base = unit + owner * extra
                for ref, start, size in ((first_ref, 0, first_size), (second_ref, first_size, second_size)):
                    at = 0
                    while at < size:
                        line, offset = divmod(start + at, cols)
                        run = min(size - at, cols - offset)
                        ref[owner : owner + 1, d * size + at : d * size + at + run] = got_ref[
                            d, base + line : base + line + 1, offset : offset + run
                        ].astype(F32)
                        at += run

    shapes = (
        jax.ShapeDtypeStruct((unit, count * cols), BF),
        jax.ShapeDtypeStruct((seqs, count * first_size), F32),
        jax.ShapeDtypeStruct((seqs, count * second_size), F32),
    )
    return pl.pallas_call(kernel, out_shape=shapes)(got)


def head_pieces(d, width, part_rows):
    at, stop = d * width, min((d + 1) * width, D)
    while at < stop:
        owner, offset = divmod(at, part_rows)
        size = min(stop - at, part_rows - offset)
        yield owner, offset, at - d * width, size
        at += size


def pack_proj(parts, row, width, count):
    part_rows, cols = parts[0].shape
    seqs = len(parts)

    def kernel(row_ref, *refs):
        parts, out_ref, held = refs[:-2], refs[-2], refs[-1]
        for step, part in enumerate(parts):
            held[step ^ row_ref[0]] = part[...]
        for d in range(count):
            for owner, offset, start, size in head_pieces(d, width, part_rows):
                out_ref[d, start : start + size, :cols] = held[owner, offset : offset + size, :]
            blank = min(width, max(0, (d + 1) * width - D))
            if blank:
                out_ref[d, width - blank :, :cols] = jnp.zeros((blank, cols), BF)

    shape = jax.ShapeDtypeStruct((count, width, lanes(cols)), BF)
    return small_kernel(kernel, shape, row, *parts, scratch=[pltpu.VMEM((seqs, part_rows, cols), BF)])


def join_columns(got, cols):
    count, rows, _ = got.shape

    def kernel(got_ref, out_ref):
        for d in range(count):
            out_ref[:, d * cols : (d + 1) * cols] = got_ref[d, :, :cols]

    return pl.pallas_call(kernel, out_shape=jax.ShapeDtypeStruct((rows, count * cols), BF))(got)


def pack_backward(out_sum, proj_grad, cols):
    unit, width = out_sum.shape[0], proj_grad.shape[0]
    count = out_sum.shape[1] // cols

    def kernel(out_ref, proj_ref, sent_ref):
        for d in range(count):
            sent_ref[d, :unit, :cols] = out_ref[:, d * cols : (d + 1) * cols]
            sent_ref[d, unit:, :cols] = proj_ref[:, d * cols : (d + 1) * cols]

    return pl.pallas_call(kernel, out_shape=jax.ShapeDtypeStruct((count, unit + width, lanes(cols)), BF))(out_sum, proj_grad)


def unpack_backward(got, row, unit, cols):
    count, total, _ = got.shape
    width, seqs = total - unit, lax.axis_size("seq")
    part_rows = D // seqs

    def kernel(row_ref, got_ref, out_ref, parts_ref, held):
        for d in range(count):
            out_ref[d * unit : (d + 1) * unit, :] = got_ref[d, :unit, :cols].astype(F32)
            for owner, offset, start, size in head_pieces(d, width, part_rows):
                held[owner, offset : offset + size, :] = got_ref[d, unit + start : unit + start + size, :cols]
        for step in range(seqs):
            parts_ref[step] = held[step ^ row_ref[0]]

    shapes = (jax.ShapeDtypeStruct((count * unit, cols), F32), jax.ShapeDtypeStruct((seqs, part_rows, cols), BF))
    return pl.pallas_call(
        kernel,
        out_shape=shapes,
        in_specs=[pl.BlockSpec(memory_space=pltpu.SMEM), pl.BlockSpec(memory_space=pltpu.VMEM)],
        out_specs=(pl.BlockSpec(memory_space=pltpu.VMEM),) * 2,
        scratch_shapes=[pltpu.VMEM((seqs, part_rows, cols), BF)],
    )(row.reshape(1), got)


def vector_at(table, start, size):
    row, offset = divmod(start, table.shape[1])
    if offset + size <= table.shape[1]:
        return table[row, offset : offset + size]
    return table.reshape(-1)[start : start + size]


def exchange(stack):
    return lax.all_to_all(stack, "ctx", split_axis=0, concat_axis=0, tiled=True)


def attention_forward(qkv, places, labels, heads):
    width, length = qkv.shape[0] // 3, qkv.shape[1]
    block = min(256, length)

    def kernel(pc_ref, lc_ref, pr_ref, lr_ref, q_ref, k_ref, v_ref, o_ref, low_ref, lse_ref, bias, keys):
        head, part = pl.program_id(0), pl.program_id(1)
        cols = pl.ds(pl.multiple_of(part * block, block), block)

        @pl.when(head == 0)
        def _():
            allowed = (pc_ref[...] <= pr_ref[:, cols]) & (lc_ref[...] == lr_ref[:, cols])
            bias[:, cols] = jnp.where(allowed, 0.0, -1e30)

        @pl.when(part == 0)
        def _():
            keys[...] = k_ref[...].T

        query = q_ref[:, cols] * BF(0.125)
        scores = mm(keys[...], query) + bias[:, cols]
        highest = jnp.max(scores, axis=0, keepdims=True)
        weights = jnp.exp(scores - highest)
        total = jnp.sum(weights, axis=0, keepdims=True)
        mixed = mm(v_ref[...], weights.astype(BF)) / total
        o_ref[:, cols] = mixed
        low_ref[:, cols] = mixed.astype(BF)
        lse_ref[0, :, cols] = highest + jnp.log(total)

    def full(shape):
        return pl.BlockSpec(shape, lambda h, p: (0,) * len(shape))

    def head_rows(offset):
        return pl.BlockSpec((HD, length), lambda h, p: (h + offset, 0))

    return pl.pallas_call(
        kernel,
        grid=(heads, length // block),
        out_shape=(
            jax.ShapeDtypeStruct((width, length), F32),
            jax.ShapeDtypeStruct((width, length), BF),
            jax.ShapeDtypeStruct((heads, 1, length), F32),
        ),
        in_specs=[full((length, 1))] * 2 + [full((1, length))] * 2 + [head_rows(0), head_rows(heads), head_rows(2 * heads)],
        out_specs=(head_rows(0), head_rows(0), pl.BlockSpec((1, 1, length), lambda h, p: (h, 0, 0))),
        scratch_shapes=[pltpu.VMEM((length, length), F32), pltpu.VMEM((length, HD), BF)],
        compiler_params=pltpu.CompilerParams(vmem_limit_bytes=VMEM_LIMIT),
        cost_estimate=pl.CostEstimate(
            flops=16 * heads * length * length * HD, bytes_accessed=12 * width * length, transcendentals=heads * length * length
        ),
    )(places[:, None], labels[:, None], places[None], labels[None], qkv, qkv, qkv)


def attention_backward(qkv, places, labels, mixed, lse, grad, heads):
    width, length = qkv.shape[0] // 3, qkv.shape[1]
    block = min(256, length)

    def kernel(pc_ref, lc_ref, pr_ref, lr_ref, q_ref, k_ref, v_ref, o_ref, lse_ref, g_ref, out_ref, bias, keys, values, dk, dv):
        head, part = pl.program_id(0), pl.program_id(1)
        cols = pl.ds(pl.multiple_of(part * block, block), block)

        @pl.when(head == 0)
        def _():
            allowed = (pc_ref[...] <= pr_ref[:, cols]) & (lc_ref[...] == lr_ref[:, cols])
            bias[:, cols] = jnp.where(allowed, 0.0, -1e30)

        @pl.when(part == 0)
        def _():
            keys[...] = k_ref[...].T
            values[...] = v_ref[...].T
            dk[...] = jnp.zeros_like(dk)
            dv[...] = jnp.zeros_like(dv)

        query = q_ref[:, cols] * BF(0.125)
        grads = g_ref[:, cols]
        delta = jnp.sum(grads.astype(F32) * o_ref[:, cols], axis=0, keepdims=True)
        scores = mm(keys[...], query) + bias[:, cols]
        prob = jnp.exp(scores - lse_ref[0, :, cols])
        prob_grad = mm(values[...], grads)
        score_grad = (prob * (prob_grad - delta)).astype(BF)
        dv[...] += mm_nt(grads, prob.astype(BF))
        dk[...] += mm_nt(query, score_grad)
        out_ref[0, :, cols] = (mm(k_ref[...], score_grad) * 0.125).astype(BF)

        @pl.when(part == pl.num_programs(1) - 1)
        def _():
            out_ref[1] = dk[...].astype(BF)
            out_ref[2] = dv[...].astype(BF)

    def full(shape):
        return pl.BlockSpec(shape, lambda h, p: (0,) * len(shape))

    def head_rows(offset):
        return pl.BlockSpec((HD, length), lambda h, p: (h + offset, 0))

    return pl.pallas_call(
        kernel,
        grid=(heads, length // block),
        out_shape=jax.ShapeDtypeStruct((3, width, length), BF),
        in_specs=[full((length, 1))] * 2
        + [full((1, length))] * 2
        + [head_rows(0), head_rows(heads), head_rows(2 * heads), head_rows(0)]
        + [pl.BlockSpec((1, 1, length), lambda h, p: (h, 0, 0)), head_rows(0)],
        out_specs=pl.BlockSpec((3, HD, length), lambda h, p: (0, h, 0)),
        scratch_shapes=[
            pltpu.VMEM((length, length), F32),
            pltpu.VMEM((length, HD), BF),
            pltpu.VMEM((length, HD), BF),
            pltpu.VMEM((HD, length), F32),
            pltpu.VMEM((HD, length), F32),
        ],
        compiler_params=pltpu.CompilerParams(vmem_limit_bytes=VMEM_LIMIT),
        cost_estimate=pl.CostEstimate(
            flops=40 * heads * length * length * HD, bytes_accessed=16 * width * length, transcendentals=heads * length * length
        ),
    )(places[:, None], labels[:, None], places[None], labels[None], qkv, qkv, qkv, mixed, lse, grad)


def seq_gather(part):
    return lax.all_gather(part, "seq", axis=0, tiled=True)


def seq_scatter(whole):
    seqs = lax.axis_size("seq")
    return lax.psum_scatter(whole.reshape(seqs, -1, whole.shape[1]), "seq", scatter_dimension=0, tiled=False)


def send_to_owner(whole):
    number, size = whole.shape
    whole = jnp.pad(whole, ((0, 0), (0, -size % 128))).reshape(number, -1, 128)
    return lax.all_to_all(whole, ("seq", "ctx"), split_axis=0, concat_axis=0, tiled=True)


def hidden_pairs(step, seqs):
    return [(2 * (v ^ step) + u, seqs * u + v) for u in range(2) for v in range(seqs)]


def hidden_forward(w_fc):
    seqs, count = lax.axis_size("seq"), lax.axis_size("ctx")
    assert count == 2 * seqs
    me = lax.axis_index("ctx")
    sent = split_columns(w_fc, seqs, me // 2)
    got = [lax.ppermute(sent[step : step + 1], "ctx", hidden_pairs(step, seqs)) for step in range(seqs)]
    return join(got, me % seqs)


def hidden_backward(grad):
    seqs = lax.axis_size("seq")
    me = lax.axis_index("ctx")
    sent = split_columns(grad, seqs, me % seqs)
    got = [
        lax.ppermute(sent[step : step + 1], "ctx", [(d, c) for c, d in hidden_pairs(step, seqs)]) for step in range(seqs)
    ]
    return join(got, me // 2, F32)


def gelu_and_grad(a):
    inner = 0.7978845608028654 * (a + 0.044715 * a * a * a)
    t = jnp.tanh(inner)
    value = 0.5 * a * (1.0 + t)
    slope = 0.5 * (1.0 + t) + 0.5 * a * (1.0 - t * t) * 0.7978845608028654 * (1.0 + 3 * 0.044715 * a * a)
    return value, slope


def normalize(values):
    average = jnp.mean(values, axis=-1, keepdims=True)
    centred = values - average
    scale = lax.rsqrt(jnp.mean(centred * centred, axis=-1, keepdims=True) + 1e-05)
    return centred * scale, scale


def norm_back(grad, gain, normed, scale):
    e = grad * gain
    return scale * (
        e - jnp.mean(e, axis=-1, keepdims=True) - normed * jnp.mean(e * normed, axis=-1, keepdims=True)
    )


def layer(tokens, cotangent, segments, block_order, w_attn, w_proj, w_fc, w_fc2, attn_vectors, other_vectors):
    seqs, count = lax.axis_size("seq"), lax.axis_size("ctx")
    me = lax.axis_index("ctx")
    rows = tokens.shape[1]
    length = rows * count
    half_block = rows // 2
    heads = -(-H // count)
    width = heads * HD
    unit = FF // (seqs * count)
    order = local_order(count)
    zero = jnp.int32(0)

    attn_cols = w_attn.shape[1]
    attn_even, attn_odd = gather_blocks(w_attn)
    wanted = jnp.arange(width, dtype=jnp.int32) + me * width
    wanted = jnp.concatenate([jnp.where(wanted < D, wanted + part * D, -1) for part in range(3)])

    def chosen(owner):
        return (jnp.arange(attn_cols, dtype=jnp.int32)[:, None] + owner * attn_cols) == wanted[None, :]

    attn_part = sum(mm(block, chosen(me ^ b).astype(BF)) for b, block in zip(order, attn_even + attn_odd)).astype(BF)
    attn_mine = seq_gather(attn_part)
    proj_cols, out_cols = w_proj.shape[1], w_fc2.shape[1]
    first_size, second_size = attn_vectors.shape[0], other_vectors.shape[0]
    row = lax.axis_index("seq")
    vectors = jnp.concatenate([attn_vectors, other_vectors])
    extra = -(-vectors.shape[0] // (8 * out_cols)) * 8
    vectors = jnp.pad(vectors, (0, extra * out_cols - vectors.shape[0])).reshape(extra, out_cols)
    vector_parts = [vectors] + [swap_seq(vectors, step) for step in range(1, seqs)]
    proj_parts = [w_proj] + [swap_seq(w_proj, step) for step in range(1, seqs)]
    fc_part = hidden_forward(w_fc)
    x_blocks = gather_start(after(tokens[0], attn_even))
    fc_mine = seq_gather(fc_part)
    packed = pack_first(w_fc2.reshape(count, unit, out_cols), vector_parts, row)
    packed = exchange(after(packed, attn_even))
    out_part, first_all, second_all = unpack_first(packed, unit, out_cols, first_size, second_size)
    out_mine = seq_gather(after(out_part, fc_part))
    x_all = gather_finish(x_blocks)
    proj_packed = pack_proj(proj_parts, row, width, count)
    proj_got = exchange(after(proj_packed, x_blocks))
    attn_mine, x_all = lax.optimization_barrier((attn_mine, x_all, fc_part, out_part, proj_packed))[:2]

    gain_one, shift_one, bias_query, bias_value = [vector_at(first_all, n * D, D) for n in range(4)]
    bias_proj, gain_two, shift_two, bias_out = [vector_at(second_all, n * D, D) for n in range(4)]
    bias_fc = vector_at(second_all, 4 * D, FF).reshape(seqs, count, unit).transpose(1, 0, 2)
    bias_fc = pick(bias_fc, me).reshape(-1)

    def my_heads(vector):
        return lax.dynamic_slice_in_dim(jnp.pad(vector, (0, count * width - D)), me * width, width)

    x_own = tokens[0].astype(F32)
    h1 = both(lambda x: (normalize(x.astype(F32))[0] * gain_one + shift_one).astype(BF), x_all)
    bias_joined = jnp.concatenate([my_heads(bias_query), jnp.zeros((width,), F32), my_heads(bias_value)])
    qkv = jnp.concatenate([(mm(h, attn_mine) + bias_joined).astype(BF) for h in h1], axis=0).T

    owners = jnp.stack([me ^ b for b in order])
    stored = (owners[:, None] * 2 + jnp.arange(2, dtype=jnp.int32)[None, :]).reshape(-1)
    blocks = jnp.take(block_order, stored)
    places = (blocks[:, None] * half_block + jnp.arange(half_block, dtype=jnp.int32)[None, :]).reshape(-1)
    labels = jnp.take(segments[0].reshape(-1, half_block), blocks, axis=0).reshape(-1)
    dy_blocks = gather_start(after(cotangent[0], x_all))
    mixed, attended, lse = attention_forward(qkv, places, labels, heads)
    proj_mine = join_columns(after(proj_got, attended), proj_cols)
    dy = gather_finish(after(dy_blocks, attended))
    half = length // 2
    attended = (attended[:, :half].T, attended[:, half:].T)
    middle = x_own + scatter_sum(attended, lambda o: mm(o, proj_mine)) + bias_proj
    normed_two, scale_two = normalize(middle)
    h2 = gather_rows((normed_two * gain_two + shift_two).astype(BF))
    active, slope = zip(*[gelu_and_grad(mm(h, fc_mine) + bias_fc) for h in h2])
    active = both(lambda g: g.astype(BF), active)

    dy_own = cotangent[0].astype(F32)
    grad_inner = both(lambda g, d: (mm_nt(g, out_mine) * d).astype(BF), dy, slope)
    grad_out_w = over_rows(active, dy).astype(BF)
    grad_fc_w = over_rows(h2, grad_inner).astype(BF)
    grad_out_w, grad_fc_w = [with_layout_constraint(g, Layout((0, 1))) for g in (grad_out_w, grad_fc_w)]
    grad_h2 = scatter_sum(grad_inner, lambda d: mm_nt(d, fc_mine), (grad_out_w, grad_fc_w))
    out_sum = seq_scatter(grad_out_w)
    fc_sum = seq_scatter(grad_fc_w)
    grad_middle = dy_own + norm_back(grad_h2, gain_two, normed_two, scale_two)
    r_blocks = gather_start(grad_middle.astype(BF))
    out_total, out_sent, out_blocks = scatter_start(after(active, r_blocks[0]), lambda g: mm(g, out_mine))
    r_all = gather_finish(after(r_blocks, out_sum, out_sent))
    grad_mixed = jnp.concatenate([mm_nt(r, proj_mine).astype(BF) for r in r_all], axis=0).T
    grad_qkv = attention_backward(qkv, places, labels, mixed, lse, grad_mixed, heads).reshape(3 * width, length)
    out_blocks, attended, r_all = lax.optimization_barrier((out_blocks, attended, r_all, grad_qkv))[:3]
    sums = jnp.sum(grad_qkv.astype(F32), axis=1)
    grad_qkv = (grad_qkv[:, :half].T, grad_qkv[:, half:].T)
    grad_attn_w = over_rows(h1, grad_qkv).astype(BF)
    attn_sum = seq_scatter(grad_attn_w)
    grad_proj_w = over_rows(after(attended, grad_attn_w), r_all).astype(BF)
    packed = pack_backward(out_sum, grad_proj_w, out_cols)
    returned = exchange(packed)
    h1_total, h1_sent, h1_blocks = scatter_start(grad_qkv, lambda d: mm_nt(after(d, grad_attn_w), attn_mine))
    output = (middle + scatter_finish(out_total, after(out_blocks, h1_sent)) + bias_out).astype(BF)
    returned = after(returned, h1_sent)
    out_own, proj_parts = unpack_backward(returned, row, unit, out_cols)
    proj_came = [swap_seq(proj_parts[step], step) for step in range(1, seqs)]
    proj_own = scatter_finish(proj_parts[0].astype(F32), proj_came)
    grad_h1 = scatter_finish(h1_total, h1_blocks)
    normed_own, scale_own = normalize(x_own)
    tokens_grad = (grad_middle + norm_back(grad_h1, gain_one, normed_own, scale_own)).astype(BF)
    fc_own = hidden_backward(after(fc_sum, h1_sent))
    attn_sum, output, proj_own, out_own, tokens_grad, fc_own = lax.optimization_barrier(
        (attn_sum, output, proj_own, out_own, tokens_grad, fc_own)
    )

    def part_for(owner, chip):
        start, stop = chip * 2 * attn_cols, (chip + 1) * 2 * attn_cols
        meets = [(owner * width + part * D < stop) & (owner * width + width + part * D > start) for part in range(3)]
        return jnp.where(meets[0], 0, jnp.where(meets[1], 1, 2))

    def part_sent(step):
        part = part_for(me, (me // 2) ^ step)
        return lax.dynamic_slice_in_dim(attn_sum, part * width, width, axis=1)

    assert 2 * attn_cols + width <= D
    attn_even = [part_sent(0)] + [swap(part_sent(step), 2 * step) for step in range(1, count // 2)]
    attn_odd = [swap(block, 1) for block in attn_even]
    attn_blocks = attn_even + attn_odd
    mine_cols = jnp.arange(attn_cols, dtype=jnp.int32) + me * attn_cols
    attn_own = jnp.zeros((attn_sum.shape[0], attn_cols), F32)
    lane = jnp.arange(width, dtype=jnp.int32)
    for b, block in zip(order, attn_blocks):
        theirs = lane + (me ^ b) * width
        theirs = jnp.where(theirs < D, theirs + part_for(me ^ b, me // 2) * D, -1)
        attn_own = attn_own + mm(block, (theirs[:, None] == mine_cols[None, :]).astype(BF))

    def head_slots(value):
        return lax.dynamic_update_slice_in_dim(jnp.zeros((count * width,), F32), value, me * width, 0)[:D]

    grad_first = jnp.concatenate(
        [
            jnp.sum(grad_h1 * normed_own, axis=0),
            jnp.sum(grad_h1, axis=0),
            head_slots(sums[:width]),
            head_slots(sums[2 * width :]),
        ]
    )
    bf_sum = sum(jnp.sum(d.astype(F32), axis=0) for d in grad_inner).reshape(seqs, 1, unit)
    bf_slots = lax.dynamic_update_slice_in_dim(jnp.zeros((seqs, count, unit), F32), bf_sum, me, 1).reshape(-1)
    grad_second = jnp.concatenate(
        [
            jnp.sum(grad_middle, axis=0),
            jnp.sum(grad_h2 * normed_two, axis=0),
            jnp.sum(grad_h2, axis=0),
            jnp.sum(dy_own, axis=0),
            bf_slots,
        ]
    )
    number = seqs * count
    own = jnp.concatenate([grad_first.reshape(number, -1), grad_second.reshape(number, -1)], axis=1)
    own = jnp.sum(after(send_to_owner(after(own, attn_sum)), attn_blocks), axis=0).reshape(-1)
    first_own, second_own = own[: attn_vectors.shape[0]], own[attn_vectors.shape[0] : attn_vectors.shape[0] + other_vectors.shape[0]]
    return (output[None], tokens_grad[None], attn_own, proj_own, fc_own, out_own, first_own, second_own)


def solution(mesh):
    rows = P("seq", "ctx", None)
    weight = P("seq", "ctx")
    vector = P(("seq", "ctx"))
    return jax.shard_map(
        layer,
        mesh=mesh,
        in_specs=(rows, rows, P("seq", None), P(), weight, weight, weight, weight, vector, vector),
        out_specs=(rows, rows, weight, weight, weight, weight, vector, vector),
        check_vma=False,
    )
```

```python
import jax
import jax.numpy as jnp
from jax import lax
from jax.experimental import pallas as pl
from jax.experimental.layout import Layout, with_layout_constraint
from jax.experimental.pallas import tpu as pltpu
from jax.sharding import PartitionSpec as P

D = 1600
FF = 6400
H = 25
HD = 64
BF = jnp.bfloat16
F32 = jnp.float32


def mm(a, b):
    return jnp.dot(a, b, preferred_element_type=F32)


def mm_nt(a, b):
    return lax.dot_general(a, b, (((1,), (1,)), ((), ())), preferred_element_type=F32)


def mm_tn(a, b):
    return lax.dot_general(a, b, (((0,), (0,)), ((), ())), preferred_element_type=F32)


def swap(value, step):
    count = lax.axis_size("ctx")
    return lax.ppermute(value, "ctx", [(i, i ^ step) for i in range(count)])


def swap_seq(value, step):
    seqs = lax.axis_size("seq")
    return lax.ppermute(value, "seq", [(i, i ^ step) for i in range(seqs)])


def local_order(count):
    return list(range(0, count, 2)) + list(range(1, count, 2))


def after(value, *others):
    return lax.optimization_barrier((value, *others))[0]


def pick(stack, number, axis=0):
    return lax.dynamic_index_in_dim(stack, number, axis, keepdims=False)


def gather_blocks(own):
    count = lax.axis_size("ctx")
    even = [own] + [swap(own, step) for step in range(2, count, 2)]
    odd = [swap(block, 1) for block in even]
    return even, odd


def gather_start(own):
    count = lax.axis_size("ctx")
    return [own] + [swap(own, step) for step in range(2, count, 2)]


def gather_finish(blocks):
    mine = jnp.concatenate(blocks, axis=0)
    return mine, swap(mine, 1)


def gather_rows(own):
    return gather_finish(gather_start(own))


def scatter_start(left, product):
    count = lax.axis_size("ctx")
    rows = left[0].shape[0] * 2 // count
    other = product(left[1]).astype(BF)
    mine = product(left[0])
    mine = mine + swap(other, 1).astype(F32)
    sent = [mine[number * rows : (number + 1) * rows].astype(BF) for number in range(1, count // 2)]
    return mine[:rows], sent, [swap(block, 2 * number) for number, block in enumerate(sent, 1)]


def scatter_finish(total, blocks):
    for block in blocks:
        total = total + block.astype(F32)
    return total


def scatter_sum(left, product, fillers=()):
    total, _, blocks = scatter_start(left, product)
    return scatter_finish(total, after(blocks, fillers) if fillers else blocks)


def both(function, *halves):
    return tuple(function(*pair) for pair in zip(*halves))


def over_rows(left, right):
    return mm_tn(left[0], right[0]) + mm_tn(left[1], right[1])


VMEM_LIMIT = 56 * 1024 * 1024


def small_kernel(kernel, shape, key, *arrays, scratch=()):
    return pl.pallas_call(
        kernel,
        out_shape=shape,
        in_specs=[pl.BlockSpec(memory_space=pltpu.SMEM)] + [pl.BlockSpec(memory_space=pltpu.VMEM)] * len(arrays),
        out_specs=pl.BlockSpec(memory_space=pltpu.VMEM),
        scratch_shapes=list(scratch),
    )(key.reshape(1), *arrays)


def split_columns(whole, number, key):
    rows, width = whole.shape[0], whole.shape[1] // number

    def kernel(key_ref, whole_ref, *refs):
        stack = refs[-1]
        for k in range(number):
            stack[k ^ key_ref[0]] = whole_ref[:, k * width : (k + 1) * width]
        for k in range(number):
            refs[k][0] = stack[k]

    return pl.pallas_call(
        kernel,
        out_shape=(jax.ShapeDtypeStruct((1, rows, width), whole.dtype),) * number,
        in_specs=[pl.BlockSpec(memory_space=pltpu.SMEM), pl.BlockSpec(memory_space=pltpu.VMEM)],
        out_specs=(pl.BlockSpec(memory_space=pltpu.VMEM),) * number,
        scratch_shapes=[pltpu.VMEM((number, rows, width), whole.dtype)],
    )(key.reshape(1), whole)


def join(parts, key, dtype=None):
    dtype = dtype or parts[0].dtype
    number = sum(part.shape[0] for part in parts)
    rows, width = parts[0].shape[1:]

    def kernel(key_ref, *refs):
        out_ref, stack = refs[-2:]
        at = 0
        for ref in refs[:-2]:
            for n in range(ref.shape[0]):
                stack[at] = ref[n]
                at += 1
        for k in range(number):
            out_ref[:, k * width : (k + 1) * width] = stack[k ^ key_ref[0]].astype(dtype)

    stack = pltpu.VMEM((number, rows, width), parts[0].dtype)
    return small_kernel(kernel, jax.ShapeDtypeStruct((rows, number * width), dtype), key, *parts, scratch=[stack])


def lanes(cols):
    return -(-cols // 128) * 128


def pack_first(out_stack, vector_parts, row):
    count, unit, cols = out_stack.shape
    seqs, extra = len(vector_parts), vector_parts[0].shape[0]

    def kernel(row_ref, stack_ref, *refs):
        parts, out_ref, held = refs[:-2], refs[-2], refs[-1]
        for step, part in enumerate(parts):
            held[step ^ row_ref[0]] = part[...]
        for d in range(count):
            out_ref[d, :unit, :cols] = stack_ref[d]
            for owner in range(seqs):
                out_ref[d, unit + owner * extra : unit + (owner + 1) * extra, :cols] = held[owner]

    shape = jax.ShapeDtypeStruct((count, unit + seqs * extra, lanes(cols)), BF)
    held = pltpu.VMEM((seqs, extra, cols), BF)
    return small_kernel(kernel, shape, row, out_stack, *vector_parts, scratch=[held])


def unpack_first(got, unit, cols, first_size, second_size):
    count, total, _ = got.shape
    seqs = lax.axis_size("seq")
    extra = (total - unit) // seqs

    def kernel(got_ref, out_ref, first_ref, second_ref):
        for d in range(count):
            out_ref[:, d * cols : (d + 1) * cols] = got_ref[d, :unit, :cols]
            for owner in range(seqs):
                base = unit + owner * extra
                for ref, start, size in ((first_ref, 0, first_size), (second_ref, first_size, second_size)):
                    at = 0
                    while at < size:
                        line, offset = divmod(start + at, cols)
                        run = min(size - at, cols - offset)
                        ref[owner : owner + 1, d * size + at : d * size + at + run] = got_ref[
                            d, base + line : base + line + 1, offset : offset + run
                        ].astype(F32)
                        at += run

    shapes = (
        jax.ShapeDtypeStruct((unit, count * cols), BF),
        jax.ShapeDtypeStruct((seqs, count * first_size), F32),
        jax.ShapeDtypeStruct((seqs, count * second_size), F32),
    )
    return pl.pallas_call(kernel, out_shape=shapes)(got)


def head_pieces(d, width, part_rows):
    at, stop = d * width, min((d + 1) * width, D)
    while at < stop:
        owner, offset = divmod(at, part_rows)
        size = min(stop - at, part_rows - offset)
        yield owner, offset, at - d * width, size
        at += size


def pack_proj(parts, row, width, count):
    part_rows, cols = parts[0].shape
    seqs = len(parts)

    def kernel(row_ref, *refs):
        parts, out_ref, held = refs[:-2], refs[-2], refs[-1]
        for step, part in enumerate(parts):
            held[step ^ row_ref[0]] = part[...]
        for d in range(count):
            for owner, offset, start, size in head_pieces(d, width, part_rows):
                out_ref[d, start : start + size, :cols] = held[owner, offset : offset + size, :]
            blank = min(width, max(0, (d + 1) * width - D))
            if blank:
                out_ref[d, width - blank :, :cols] = jnp.zeros((blank, cols), BF)

    shape = jax.ShapeDtypeStruct((count, width, lanes(cols)), BF)
    return small_kernel(kernel, shape, row, *parts, scratch=[pltpu.VMEM((seqs, part_rows, cols), BF)])


def join_columns(got, cols):
    count, rows, _ = got.shape

    def kernel(got_ref, out_ref):
        for d in range(count):
            out_ref[:, d * cols : (d + 1) * cols] = got_ref[d, :, :cols]

    return pl.pallas_call(kernel, out_shape=jax.ShapeDtypeStruct((rows, count * cols), BF))(got)


def pack_backward(out_sum, proj_grad, cols):
    unit, width = out_sum.shape[0], proj_grad.shape[0]
    count = out_sum.shape[1] // cols

    def kernel(out_ref, proj_ref, sent_ref):
        for d in range(count):
            sent_ref[d, :unit, :cols] = out_ref[:, d * cols : (d + 1) * cols]
            sent_ref[d, unit:, :cols] = proj_ref[:, d * cols : (d + 1) * cols]

    return pl.pallas_call(kernel, out_shape=jax.ShapeDtypeStruct((count, unit + width, lanes(cols)), BF))(out_sum, proj_grad)


def unpack_backward(got, row, unit, cols):
    count, total, _ = got.shape
    width, seqs = total - unit, lax.axis_size("seq")
    part_rows = D // seqs

    def kernel(row_ref, got_ref, out_ref, *refs):
        held = refs[-1]
        for d in range(count):
            out_ref[d * unit : (d + 1) * unit, :] = got_ref[d, :unit, :cols].astype(F32)
            for owner, offset, start, size in head_pieces(d, width, part_rows):
                held[owner, offset : offset + size, :] = got_ref[d, unit + start : unit + start + size, :cols]
        for step in range(seqs):
            refs[step][...] = held[step ^ row_ref[0]]

    shapes = (jax.ShapeDtypeStruct((count * unit, cols), F32),) + (jax.ShapeDtypeStruct((part_rows, cols), BF),) * seqs
    return pl.pallas_call(
        kernel,
        out_shape=shapes,
        in_specs=[pl.BlockSpec(memory_space=pltpu.SMEM), pl.BlockSpec(memory_space=pltpu.VMEM)],
        out_specs=(pl.BlockSpec(memory_space=pltpu.VMEM),) * (1 + seqs),
        scratch_shapes=[pltpu.VMEM((seqs, part_rows, cols), BF)],
    )(row.reshape(1), got)


def vector_at(table, start, size):
    row, offset = divmod(start, table.shape[1])
    if offset + size <= table.shape[1]:
        return table[row, offset : offset + size]
    return table.reshape(-1)[start : start + size]


def exchange(stack):
    return lax.all_to_all(stack, "ctx", split_axis=0, concat_axis=0, tiled=True)


def attention_specs(length, heads):
    half = length // 2

    def full(shape):
        return pl.BlockSpec(shape, lambda h, p: (0,) * len(shape))

    def head_rows(part, size):
        return pl.BlockSpec((HD, size), lambda h, p: (h + part * heads, 0))

    places = [full((length, 1))] * 2 + [full((1, length))] * 2
    qkv = [head_rows(part, half) for part in range(3) for _ in range(2)]
    return places, qkv, head_rows, pl.BlockSpec((1, 1, length), lambda h, p: (h, 0, 0))


def in_half(part, block, half, action):
    per = half // block
    for side in range(2):

        @pl.when(part // per == side)
        def _():
            action(side, pl.ds(pl.multiple_of((part - side * per) * block, block), block))


def attention_forward(qkv, places, labels, heads):
    width, half = qkv[0].shape[0] // 3, qkv[0].shape[1]
    length = 2 * half
    block = min(256, half)

    def kernel(pc_ref, lc_ref, pr_ref, lr_ref, q0, q1, k0, k1, v0, v1, o_ref, low0, low1, lse_ref, bias, queries, keys, values):
        head, part = pl.program_id(0), pl.program_id(1)
        cols = pl.ds(pl.multiple_of(part * block, block), block)

        @pl.when(head == 0)
        def _():
            allowed = (pc_ref[...] <= pr_ref[:, cols]) & (lc_ref[...] == lr_ref[:, cols])
            bias[:, cols] = jnp.where(allowed, 0.0, -1e30)

        @pl.when(part == 0)
        def _():
            for side, (q, k, v) in enumerate(((q0, k0, v0), (q1, k1, v1))):
                at = slice(side * half, (side + 1) * half)
                queries[:, at] = q[...] * BF(0.125)
                keys[at, :] = k[...].T
                values[:, at] = v[...]

        scores = mm(keys[...], queries[:, cols]) + bias[:, cols]
        highest = jnp.max(scores, axis=0, keepdims=True)
        weights = jnp.exp(scores - highest)
        total = jnp.sum(weights, axis=0, keepdims=True)
        mixed = mm(values[...], weights.astype(BF)) / total
        o_ref[:, cols] = mixed
        lse_ref[0, :, cols] = highest + jnp.log(total)

        def keep(side, columns):
            (low0, low1)[side][:, columns] = mixed.astype(BF)

        in_half(part, block, half, keep)

    specs, qkv_specs, head_rows, row = attention_specs(length, heads)
    return pl.pallas_call(
        kernel,
        grid=(heads, length // block),
        out_shape=(
            jax.ShapeDtypeStruct((width, length), F32),
            jax.ShapeDtypeStruct((width, half), BF),
            jax.ShapeDtypeStruct((width, half), BF),
            jax.ShapeDtypeStruct((heads, 1, length), F32),
        ),
        in_specs=specs + qkv_specs,
        out_specs=(head_rows(0, length), head_rows(0, half), head_rows(0, half), row),
        scratch_shapes=[
            pltpu.VMEM((length, length), F32),
            pltpu.VMEM((HD, length), BF),
            pltpu.VMEM((length, HD), BF),
            pltpu.VMEM((HD, length), BF),
        ],
        compiler_params=pltpu.CompilerParams(vmem_limit_bytes=VMEM_LIMIT),
        cost_estimate=pl.CostEstimate(
            flops=16 * heads * length * length * HD, bytes_accessed=12 * width * length, transcendentals=heads * length * length
        ),
    )(places[:, None], labels[:, None], places[None], labels[None], *(qkv * 3))


def attention_backward(qkv, places, labels, mixed, lse, grad, heads):
    width, half = qkv[0].shape[0] // 3, qkv[0].shape[1]
    length = 2 * half
    block = min(256, half)

    def kernel(pc_ref, lc_ref, pr_ref, lr_ref, q0, q1, k0, k1, v0, v1, o_ref, lse_ref, g0, g1, *rest):
        out0, out1, bias, queries, turned, keys, values, grads_all, dk, dv = rest
        head, part = pl.program_id(0), pl.program_id(1)
        cols = pl.ds(pl.multiple_of(part * block, block), block)

        @pl.when(head == 0)
        def _():
            allowed = (pc_ref[...] <= pr_ref[:, cols]) & (lc_ref[...] == lr_ref[:, cols])
            bias[:, cols] = jnp.where(allowed, 0.0, -1e30)

        @pl.when(part == 0)
        def _():
            for side, (q, k, v, g) in enumerate(((q0, k0, v0, g0), (q1, k1, v1, g1))):
                at = slice(side * half, (side + 1) * half)
                queries[:, at] = q[...] * BF(0.125)
                turned[:, at] = k[...]
                keys[at, :] = k[...].T
                values[at, :] = v[...].T
                grads_all[:, at] = g[...]
            dk[...] = jnp.zeros_like(dk)
            dv[...] = jnp.zeros_like(dv)

        query = queries[:, cols]
        grads = grads_all[:, cols]
        delta = jnp.sum(grads.astype(F32) * o_ref[:, cols], axis=0, keepdims=True)
        scores = mm(keys[...], query) + bias[:, cols]
        prob = jnp.exp(scores - lse_ref[0, :, cols])
        prob_grad = mm(values[...], grads)
        score_grad = (prob * (prob_grad - delta)).astype(BF)
        dv[...] += mm_nt(grads, prob.astype(BF))
        dk[...] += mm_nt(query, score_grad)
        dq = (mm(turned[...], score_grad) * 0.125).astype(BF)

        def keep(side, columns):
            (out0, out1)[side][0, :, columns] = dq

        in_half(part, block, half, keep)

        @pl.when(part == pl.num_programs(1) - 1)
        def _():
            for side, out in enumerate((out0, out1)):
                at = slice(side * half, (side + 1) * half)
                out[1] = dk[:, at].astype(BF)
                out[2] = dv[:, at].astype(BF)

    specs, qkv_specs, head_rows, row = attention_specs(length, heads)
    out_spec = pl.BlockSpec((3, HD, half), lambda h, p: (0, h, 0))
    return pl.pallas_call(
        kernel,
        grid=(heads, length // block),
        out_shape=(jax.ShapeDtypeStruct((3, width, half), BF),) * 2,
        in_specs=specs + qkv_specs + [head_rows(0, length), row, head_rows(0, half), head_rows(0, half)],
        out_specs=(out_spec, out_spec),
        scratch_shapes=[
            pltpu.VMEM((length, length), F32),
            pltpu.VMEM((HD, length), BF),
            pltpu.VMEM((HD, length), BF),
            pltpu.VMEM((length, HD), BF),
            pltpu.VMEM((length, HD), BF),
            pltpu.VMEM((HD, length), BF),
            pltpu.VMEM((HD, length), F32),
            pltpu.VMEM((HD, length), F32),
        ],
        compiler_params=pltpu.CompilerParams(vmem_limit_bytes=VMEM_LIMIT),
        cost_estimate=pl.CostEstimate(
            flops=40 * heads * length * length * HD, bytes_accessed=16 * width * length, transcendentals=heads * length * length
        ),
    )(places[:, None], labels[:, None], places[None], labels[None], *(qkv * 3), mixed, lse, *grad)


def seq_gather(part):
    return lax.all_gather(part, "seq", axis=0, tiled=True)


def seq_scatter(whole):
    seqs = lax.axis_size("seq")
    return lax.psum_scatter(whole.reshape(seqs, -1, whole.shape[1]), "seq", scatter_dimension=0, tiled=False)


def send_to_owner(whole):
    number, size = whole.shape
    whole = jnp.pad(whole, ((0, 0), (0, -size % 128))).reshape(number, -1, 128)
    return lax.all_to_all(whole, ("seq", "ctx"), split_axis=0, concat_axis=0, tiled=True)


def hidden_pairs(step, seqs):
    return [(2 * (v ^ step) + u, seqs * u + v) for u in range(2) for v in range(seqs)]


def hidden_forward(w_fc):
    seqs, count = lax.axis_size("seq"), lax.axis_size("ctx")
    assert count == 2 * seqs
    me = lax.axis_index("ctx")
    sent = split_columns(w_fc, seqs, me // 2)
    got = [lax.ppermute(sent[step], "ctx", hidden_pairs(step, seqs)) for step in range(seqs)]
    return join(got, me % seqs)


def hidden_backward(grad):
    seqs = lax.axis_size("seq")
    me = lax.axis_index("ctx")
    sent = split_columns(grad, seqs, me % seqs)
    got = [
        lax.ppermute(sent[step], "ctx", [(d, c) for c, d in hidden_pairs(step, seqs)]) for step in range(seqs)
    ]
    return join(got, me // 2, F32)


def gelu_and_grad(a):
    inner = 0.7978845608028654 * (a + 0.044715 * a * a * a)
    t = jnp.tanh(inner)
    value = 0.5 * a * (1.0 + t)
    slope = 0.5 * (1.0 + t) + 0.5 * a * (1.0 - t * t) * 0.7978845608028654 * (1.0 + 3 * 0.044715 * a * a)
    return value, slope


def normalize(values):
    average = jnp.mean(values, axis=-1, keepdims=True)
    centred = values - average
    scale = lax.rsqrt(jnp.mean(centred * centred, axis=-1, keepdims=True) + 1e-05)
    return centred * scale, scale


def norm_back(grad, gain, normed, scale):
    e = grad * gain
    return scale * (
        e - jnp.mean(e, axis=-1, keepdims=True) - normed * jnp.mean(e * normed, axis=-1, keepdims=True)
    )


def layer(tokens, cotangent, segments, block_order, w_attn, w_proj, w_fc, w_fc2, attn_vectors, other_vectors):
    seqs, count = lax.axis_size("seq"), lax.axis_size("ctx")
    me = lax.axis_index("ctx")
    rows = tokens.shape[1]
    half_block = rows // 2
    heads = -(-H // count)
    width = heads * HD
    unit = FF // (seqs * count)
    order = local_order(count)
    zero = jnp.int32(0)

    attn_cols = w_attn.shape[1]
    attn_even, attn_odd = gather_blocks(w_attn)
    wanted = jnp.arange(width, dtype=jnp.int32) + me * width
    wanted = jnp.concatenate([jnp.where(wanted < D, wanted + part * D, -1) for part in range(3)])

    def chosen(owner):
        return (jnp.arange(attn_cols, dtype=jnp.int32)[:, None] + owner * attn_cols) == wanted[None, :]

    attn_part = sum(mm(block, chosen(me ^ b).astype(BF)) for b, block in zip(order, attn_even + attn_odd)).astype(BF)
    attn_mine = seq_gather(attn_part)
    proj_cols, out_cols = w_proj.shape[1], w_fc2.shape[1]
    first_size, second_size = attn_vectors.shape[0], other_vectors.shape[0]
    row = lax.axis_index("seq")
    vectors = jnp.concatenate([attn_vectors, other_vectors])
    extra = -(-vectors.shape[0] // (8 * out_cols)) * 8
    vectors = jnp.pad(vectors, (0, extra * out_cols - vectors.shape[0])).reshape(extra, out_cols)
    vector_parts = [vectors] + [swap_seq(vectors, step) for step in range(1, seqs)]
    proj_parts = [w_proj] + [swap_seq(w_proj, step) for step in range(1, seqs)]
    fc_part = hidden_forward(w_fc)
    x_blocks = gather_start(after(tokens[0], attn_even))
    fc_mine = seq_gather(fc_part)
    packed = pack_first(w_fc2.reshape(count, unit, out_cols), vector_parts, row)
    packed = exchange(after(packed, attn_even))
    out_part, first_all, second_all = unpack_first(packed, unit, out_cols, first_size, second_size)
    out_mine = seq_gather(after(out_part, fc_part))
    proj_packed = pack_proj(proj_parts, row, width, count)
    proj_got = exchange(after(proj_packed, x_blocks))
    x_all = gather_finish(after(x_blocks, proj_packed))
    attn_mine, x_all = lax.optimization_barrier((attn_mine, x_all, fc_part, out_part))[:2]

    gain_one, shift_one, bias_query, bias_value = [vector_at(first_all, n * D, D) for n in range(4)]
    bias_proj, gain_two, shift_two, bias_out = [vector_at(second_all, n * D, D) for n in range(4)]
    bias_fc = vector_at(second_all, 4 * D, FF).reshape(seqs, count, unit).transpose(1, 0, 2)
    bias_fc = pick(bias_fc, me).reshape(-1)

    def my_heads(vector):
        return lax.dynamic_slice_in_dim(jnp.pad(vector, (0, count * width - D)), me * width, width)

    x_own = tokens[0].astype(F32)
    h1 = both(lambda x: (normalize(x.astype(F32))[0] * gain_one + shift_one).astype(BF), x_all)
    bias_joined = jnp.concatenate([my_heads(bias_query), jnp.zeros((width,), F32), my_heads(bias_value)])
    qkv = tuple((mm(h, attn_mine) + bias_joined).astype(BF).T for h in h1)

    owners = jnp.stack([me ^ b for b in order])
    stored = (owners[:, None] * 2 + jnp.arange(2, dtype=jnp.int32)[None, :]).reshape(-1)
    blocks = jnp.take(block_order, stored)
    places = (blocks[:, None] * half_block + jnp.arange(half_block, dtype=jnp.int32)[None, :]).reshape(-1)
    labels = jnp.take(segments[0].reshape(-1, half_block), blocks, axis=0).reshape(-1)
    dy_blocks = gather_start(after(cotangent[0], x_all))
    mixed, low_first, low_second, lse = attention_forward(qkv, places, labels, heads)
    attended = (low_first.T, low_second.T)
    proj_mine = join_columns(after(proj_got, attended), proj_cols)
    dy = gather_finish(after(dy_blocks, attended))
    middle = x_own + scatter_sum(attended, lambda o: mm(o, proj_mine)) + bias_proj
    normed_two, scale_two = normalize(middle)
    h2 = gather_rows((normed_two * gain_two + shift_two).astype(BF))
    active, slope = zip(*[gelu_and_grad(mm(h, fc_mine) + bias_fc) for h in h2])
    active = both(lambda g: g.astype(BF), active)

    dy_own = cotangent[0].astype(F32)
    grad_out_w = over_rows(active, dy).astype(BF)
    grad_inner = both(lambda g, d: (mm_nt(g, out_mine) * d).astype(BF), after(dy, grad_out_w), slope)
    grad_fc_w = over_rows(h2, grad_inner).astype(BF)
    grad_out_w, grad_fc_w = [with_layout_constraint(g, Layout((0, 1))) for g in (grad_out_w, grad_fc_w)]
    grad_h2 = scatter_sum(grad_inner, lambda d: mm_nt(d, fc_mine), (grad_out_w, grad_fc_w))
    out_sum = seq_scatter(grad_out_w)
    fc_sum = seq_scatter(grad_fc_w)
    grad_middle = dy_own + norm_back(grad_h2, gain_two, normed_two, scale_two)
    r_blocks = gather_start(grad_middle.astype(BF))
    out_total, out_sent, out_blocks = scatter_start(after(active, r_blocks[0]), lambda g: mm(g, out_mine))
    r_all = gather_finish(after(r_blocks, out_sum, out_sent))
    grad_mixed = tuple(mm_nt(r, proj_mine).astype(BF).T for r in r_all)
    grad_qkv = attention_backward(qkv, places, labels, mixed, lse, grad_mixed, heads)
    grad_qkv = tuple(grad.reshape(3 * width, -1) for grad in grad_qkv)
    out_blocks, attended, r_all = lax.optimization_barrier((out_blocks, attended, r_all, grad_qkv))[:3]
    sums = sum(jnp.sum(grad.astype(F32), axis=1) for grad in grad_qkv)
    grad_qkv = tuple(grad.T for grad in grad_qkv)
    grad_attn_w = over_rows(h1, grad_qkv).astype(BF)
    attn_sum = seq_scatter(grad_attn_w)
    grad_proj_w = over_rows(after(attended, grad_attn_w), r_all).astype(BF)
    packed = pack_backward(out_sum, grad_proj_w, out_cols)
    returned = exchange(packed)
    h1_total, h1_sent, h1_blocks = scatter_start(grad_qkv, lambda d: mm_nt(after(d, grad_attn_w), attn_mine))
    output = (middle + scatter_finish(out_total, after(out_blocks, h1_sent)) + bias_out).astype(BF)
    returned = after(returned, h1_sent)
    out_own, *proj_parts = unpack_backward(returned, row, unit, out_cols)
    proj_came = [swap_seq(proj_parts[step], step) for step in range(1, seqs)]
    proj_own = scatter_finish(proj_parts[0].astype(F32), proj_came)
    grad_h1 = scatter_finish(h1_total, h1_blocks)
    normed_own, scale_own = normalize(x_own)
    tokens_grad = (grad_middle + norm_back(grad_h1, gain_one, normed_own, scale_own)).astype(BF)
    fc_own = hidden_backward(after(fc_sum, h1_sent))
    attn_sum, output, proj_own, out_own = lax.optimization_barrier((attn_sum, output, proj_own, out_own))

    def part_for(owner, chip):
        start, stop = chip * 2 * attn_cols, (chip + 1) * 2 * attn_cols
        meets = [(owner * width + part * D < stop) & (owner * width + width + part * D > start) for part in range(3)]
        return jnp.where(meets[0], 0, jnp.where(meets[1], 1, 2))

    def part_sent(step):
        part = part_for(me, (me // 2) ^ step)
        return lax.dynamic_slice_in_dim(attn_sum, part * width, width, axis=1)

    assert 2 * attn_cols + width <= D
    attn_even = [part_sent(0)] + [swap(part_sent(step), 2 * step) for step in range(1, count // 2)]
    attn_odd = [swap(block, 1) for block in attn_even]
    attn_blocks = attn_even + attn_odd
    mine_cols = jnp.arange(attn_cols, dtype=jnp.int32) + me * attn_cols
    attn_own = jnp.zeros((attn_sum.shape[0], attn_cols), F32)
    lane = jnp.arange(width, dtype=jnp.int32)
    for b, block in zip(order, attn_blocks):
        theirs = lane + (me ^ b) * width
        theirs = jnp.where(theirs < D, theirs + part_for(me ^ b, me // 2) * D, -1)
        attn_own = attn_own + mm(block, (theirs[:, None] == mine_cols[None, :]).astype(BF))

    def head_slots(value):
        return lax.dynamic_update_slice_in_dim(jnp.zeros((count * width,), F32), value, me * width, 0)[:D]

    grad_first = jnp.concatenate(
        [
            jnp.sum(grad_h1 * normed_own, axis=0),
            jnp.sum(grad_h1, axis=0),
            head_slots(sums[:width]),
            head_slots(sums[2 * width :]),
        ]
    )
    bf_sum = sum(jnp.sum(d.astype(F32), axis=0) for d in grad_inner).reshape(seqs, 1, unit)
    bf_slots = lax.dynamic_update_slice_in_dim(jnp.zeros((seqs, count, unit), F32), bf_sum, me, 1).reshape(-1)
    grad_second = jnp.concatenate(
        [
            jnp.sum(grad_middle, axis=0),
            jnp.sum(grad_h2 * normed_two, axis=0),
            jnp.sum(grad_h2, axis=0),
            jnp.sum(dy_own, axis=0),
            bf_slots,
        ]
    )
    number = seqs * count
    own = jnp.concatenate([grad_first.reshape(number, -1), grad_second.reshape(number, -1)], axis=1)
    own = jnp.sum(after(send_to_owner(after(own, attn_even[:2])), attn_odd), axis=0).reshape(-1)
    first_own, second_own = own[: attn_vectors.shape[0]], own[attn_vectors.shape[0] : attn_vectors.shape[0] + other_vectors.shape[0]]
    return (output[None], tokens_grad[None], attn_own, proj_own, fc_own, out_own, first_own, second_own)


def solution(mesh):
    rows = P("seq", "ctx", None)
    weight = P("seq", "ctx")
    vector = P(("seq", "ctx"))
    return jax.shard_map(
        layer,
        mesh=mesh,
        in_specs=(rows, rows, P("seq", None), P(), weight, weight, weight, weight, vector, vector),
        out_specs=(rows, rows, weight, weight, weight, weight, vector, vector),
        check_vma=False,
    )
```
